32 devices in a mesh: dom: 8 (over z, core), seg: 4 (over y, x).
Axes of the slice: x: 2, y: 2, z: 4, core: 2. Of those that a mesh axis runs over, the one named last changes fastest.
Arguments:
- state: float32 [256, 9, 64], P(('dom', 'seg'))
- counts: int32 [256], P(('dom', 'seg')), may hold values from 16 to 64
- neighbours: int32 [256, 26], P(('dom', 'seg')), may hold values from 0 to 95, as said below
- new_place: int32 [256], P(('dom', 'seg')), may hold values from 0 to 31, as said below
Outputs:
- moved_state: float32 [256, 9, 64], P(('dom', 'seg'))
- moved_density: float32 [256, 64], P(('dom', 'seg'))
The draws below stay inside these ranges and needn't reach their ends.
Inputs may be any that keep to these rules, and one draw needn't show every extreme that they name: `neighbours`: each row lists 26 distinct region indices in 0 to 95, never the block's own index 32 + k. `new_place`: within each domain range the 32 values are a permutation.
All inputs are finite; a program needn't handle non-finite values.
Results may differ from the reference program's by a relative error of at most 0.00002.
Values sent between devices are 32-bit elements; how exact they have to be, the bound alone decides.
No kernel may reach another device: no remote copies, remote signals or barrier semaphores. Data moves between devices by JAX's collectives and lax.ppermute only.
A program may use at most 64 MiB of HBM per device.

```python
import math
import jax
import jax.numpy as jnp
from jax import lax

P_SIZE = 64
NBR = 26
SLAB = 32
NB = 256


def draw_state(key, part):
    keys = jax.random.split(jax.random.fold_in(key, 11), 5)
    position = jax.random.normal(keys[0], (NB, 3, P_SIZE), jnp.float32)
    velocity = 0.5 * jax.random.normal(keys[1], (NB, 3, P_SIZE), jnp.float32)
    mass = jnp.exp(jax.random.uniform(keys[2], (NB, 1, P_SIZE), jnp.float32, jnp.log(0.2), jnp.log(2.0)))
    smooth = jnp.exp(jax.random.uniform(keys[3], (NB, 1, P_SIZE), jnp.float32, jnp.log(0.6), jnp.log(1.2)))
    energy = jnp.exp(jax.random.uniform(keys[4], (NB, 1, P_SIZE), jnp.float32, jnp.log(0.2), jnp.log(3.0)))
    return jnp.concatenate([position, velocity, mass, smooth, energy], axis=1)


def draw_neighbours(key, part):
    rows = jnp.arange(NB, dtype=jnp.int32)
    region = 3 * SLAB
    scores = jax.random.randint(jax.random.fold_in(key, 23), (NB, region), 0, 1 << 20, dtype=jnp.int32)
    columns = jnp.arange(region, dtype=jnp.int32)
    scores = scores * 512 + columns[None, :]
    self_column = SLAB + rows % SLAB
    scores = jnp.where(columns[None, :] == self_column[:, None], -1, scores)
    return lax.top_k(scores, NBR)[1].astype(jnp.int32)


def draw_new_place(key, part):
    ranges = NB // SLAB
    keys = jax.random.split(jax.random.fold_in(key, 37), ranges)
    places = jax.vmap(lambda k: jax.random.permutation(k, SLAB))(keys)
    return places.reshape(-1).astype(jnp.int32)


def touch_ends(drawn, rng, smallest, high):
    longest = drawn.shape.index(max(drawn.shape))
    spots = []
    for shift in (0, 1):
        where = [jax.random.randint(jax.random.fold_in(rng, axis), (), 0, length) for axis, length in enumerate(drawn.shape)]
        where[longest] = (where[longest] + shift) % drawn.shape[longest]
        spots.append(tuple(where))
    return drawn.at[spots[0]].set(smallest).at[spots[1]].set(high)


def setup_inputs(seed: int = 0) -> dict:
    splits = jax.random.split(jax.random.key(seed), 5)
    state = draw_state(jax.random.fold_in(splits[4], 71), 0)
    counts = touch_ends(jax.random.randint(splits[1], (NB,), P_SIZE // 4, P_SIZE + 1), jax.random.fold_in(splits[1], 1), P_SIZE // 4, P_SIZE).astype(jnp.int32)
    neighbours = draw_neighbours(jax.random.fold_in(splits[4], 71), 0)
    new_place = draw_new_place(jax.random.fold_in(splits[4], 71), 0)
    return dict(state=state, counts=counts, neighbours=neighbours, new_place=new_place)


SIGMA = 21.0 / (16.0 * math.pi)
GAMMA_LESS = 2.0 / 3.0
STEP_DT = 0.1

def offsets(own_pos, far_pos):
    return own_pos[:, :, None] - far_pos[:, None, :]

def density_tile(own, far):
    diff = offsets(own[0:3], far[0:3])
    dist = jnp.sqrt(lax.optimization_barrier(jnp.sum(diff * diff, axis=0)))
    smooth = own[7][:, None]
    ratio = dist / smooth
    shell = jnp.maximum(1.0 - 0.5 * ratio, 0.0)
    kernel = SIGMA / smooth ** 3 * shell ** 4 * (1.0 + 2.0 * ratio)
    return lax.optimization_barrier(jnp.sum(kernel * far[6][None, :], axis=1))

def slope(own, far):
    diff = offsets(own[0:3], far[0:3])
    dist = jnp.sqrt(lax.optimization_barrier(jnp.sum(diff * diff, axis=0)))
    smooth = 0.5 * (own[7][:, None] + far[7][None, :])
    ratio = dist / smooth
    shell = jnp.maximum(1.0 - 0.5 * ratio, 0.0)
    factor = -5.0 * SIGMA / smooth ** 5 * shell ** 3
    return (diff, factor)

def tensor_tile(own, far, far_vol):
    diff, factor = slope(own, far)
    weight = -factor * far_vol[None, :]
    pairs = ((0, 0), (1, 1), (2, 2), (0, 1), (0, 2), (1, 2))
    return jnp.stack([lax.optimization_barrier(jnp.sum(weight * diff[a] * diff[b], axis=1)) for a, b in pairs])

def corrected(tensor):
    return jnp.stack([2.0 - tensor[0], 2.0 - tensor[1], 2.0 - tensor[2], -tensor[3], -tensor[4], -tensor[5]])

def apply_sym(sym, vec):
    first = sym[0] * vec[0] + sym[3] * vec[1] + sym[4] * vec[2]
    second = sym[3] * vec[0] + sym[1] * vec[1] + sym[5] * vec[2]
    third = sym[4] * vec[0] + sym[5] * vec[1] + sym[2] * vec[2]
    return jnp.stack([first, second, third])

def momentum_tile(own, own_corr, own_press, far, far_corr, far_press):
    diff, factor = slope(own, far)
    scaled = diff * factor[None]
    grad_own = apply_sym(own_corr[:, :, None], scaled)
    grad_far = apply_sym(far_corr[:, None, :], scaled)
    mass_far = far[6][None, :]
    accel = -lax.optimization_barrier(jnp.sum(mass_far[None] * (own_press[None, :, None] * grad_own + far_press[None, None, :] * grad_far), axis=2))
    dvel = own[3:6][:, :, None] - far[3:6][:, None, :]
    heat = own_press * lax.optimization_barrier(jnp.sum(mass_far * lax.optimization_barrier(jnp.sum(dvel * grad_own, axis=0)), axis=1))
    return (accel, heat)

def tile_of(padded, index):
    tile = padded[index]
    if tile.ndim == 3:
        return jnp.moveaxis(tile, 0, 1).reshape(tile.shape[1], -1)
    return tile.reshape(-1)

def reference(state, counts, neighbours, new_place):
    total = state.shape[0]
    width = state.shape[2]
    live = (jnp.arange(width, dtype=jnp.int32)[None, :] < counts[:, None]).astype(jnp.float32)
    base = jnp.concatenate([state[:, 0:6], (state[:, 6] * live)[:, None], state[:, 7:9]], axis=1)
    rows = jnp.arange(total, dtype=jnp.int32)
    lists = jnp.concatenate([(SLAB + rows % SLAB)[:, None], neighbours], axis=1)
    glob = ((rows // SLAB)[:, None] * SLAB + lists).astype(jnp.int32)

    def pad(values):
        zeros = jnp.zeros((SLAB,) + values.shape[1:], values.dtype)
        return jnp.concatenate([zeros, values, zeros], axis=0)
    padded_state = pad(base)

    def first(r):
        return density_tile(base[r], tile_of(padded_state, glob[r]))
    rho = lax.map(first, rows) + (1.0 - live)
    vol = base[:, 6] / rho
    padded_vol = pad(vol)

    def second(r):
        return tensor_tile(base[r], tile_of(padded_state, glob[r]), tile_of(padded_vol, glob[r]))
    corr = corrected(jnp.moveaxis(lax.map(second, rows), 1, 0))
    corr = jnp.moveaxis(corr, 0, 1)
    press = GAMMA_LESS * base[:, 8] / rho
    extra = jnp.concatenate([corr, press[:, None]], axis=1)
    padded_extra = pad(extra)

    def third(r):
        far_extra = tile_of(padded_extra, glob[r])
        return momentum_tile(base[r], corr[r], press[r], tile_of(padded_state, glob[r]), far_extra[0:6], far_extra[6])
    accel, heat = lax.map(third, rows)
    accel = accel * live[:, None]
    heat = heat * live
    velocity = state[:, 3:6] + STEP_DT * accel
    position = state[:, 0:3] + STEP_DT * velocity
    energy = state[:, 8] + STEP_DT * heat
    updated = jnp.concatenate([position, velocity, state[:, 6:8], energy[:, None]], axis=1)
    dest = (rows // SLAB * SLAB + new_place).astype(jnp.int32)
    moved_state = jnp.zeros_like(updated).at[dest].set(updated)
    moved_density = jnp.zeros_like(rho).at[dest].set(rho)
    return (moved_state, moved_density)
```

```python
import functools
import math

import jax
import jax.numpy as jnp
from jax import lax
from jax.experimental import pallas as pl
from jax.experimental.pallas import tpu as pltpu
from jax.sharding import PartitionSpec as P

SIGMA = 21.0 / (16.0 * math.pi)
GAMMA_LESS = 2.0 / 3.0
STEP_DT = 0.1
SLOPE = -5.0 * SIGMA * 32.0
TINY = 1e-37
SUB = 8
LANES = 128
X, VEL, MASS, SMOOTH = 0, 3, 6, 7
VMEM = pltpu.VMEM
SMEM = pltpu.SMEM


def lane_iota(rows=SUB):
    return lax.broadcasted_iota(jnp.int32, (rows, LANES), 1)


def row_iota(rows=SUB):
    return lax.broadcasted_iota(jnp.int32, (rows, LANES), 0)


def call(body, outs, scratch=(), in_specs=None, out_specs=None, name=None):
    return pl.pallas_call(
        body,
        out_shape=outs,
        in_specs=in_specs,
        out_specs=out_specs,
        scratch_shapes=list(scratch),
        compiler_params=pltpu.CompilerParams(vmem_limit_bytes=56 << 20),
        name=name,
    )


def shape(*dims, dtype=jnp.float32):
    return jax.ShapeDtypeStruct(dims, dtype)


def pack_body(blocks, width, nbr, counts, place, state, lists, out):
    pairs = blocks // 2
    lane = lane_iota()
    row = row_iota()
    low = lane < width
    meta = jnp.concatenate(
        [lists[...].astype(jnp.float32), jnp.zeros((blocks, LANES - nbr), jnp.float32)], axis=1
    )
    for b in range(blocks):
        meta = jnp.where((row == b) & (lane == nbr), place[b].astype(jnp.float32), meta)
    base = pairs * SUB
    out[base : base + SUB, :] = meta
    for p in range(pairs):
        full = jnp.concatenate([state[2 * p], state[2 * p + 1]], axis=1)
        live = lane < jnp.where(low, counts[2 * p], counts[2 * p + 1] + width)
        tile = full[0:SUB]
        out[p * SUB : (p + 1) * SUB, :] = jnp.where((row == MASS) & jnp.logical_not(live), 0.0, tile)
        out[base + SUB + p : base + SUB + p + 1, :] = full[8:9]
        out[base + SUB + pairs + p : base + SUB + pairs + p + 1, :] = full[MASS : MASS + 1]
        out[base + 2 * SUB + p : base + 2 * SUB + p + 1, :] = jnp.where(live, 1.0, 0.0)[0:1]
    out[base + 2 * SUB + pairs : base + 3 * SUB, :] = jnp.zeros((SUB - pairs, LANES), jnp.float32)


def range_bases(slab):
    odd = lax.rem(lax.axis_index("dom"), 2)
    first = jnp.where(odd == 0, 2 * slab, 0)
    second = jnp.where(odd == 0, 0, 2 * slab)
    return first, second


def spread_tile(tile, width):
    low = lane_iota(tile.shape[0]) < width
    turned = pltpu.roll(tile, width, axis=1)
    return jnp.where(low, tile, turned), jnp.where(low, turned, tile)


def far_pair(left, right):
    return jnp.where(lane_iota(left.shape[0]) < LANES // 2, left, right)


def column(value, index):
    return jnp.broadcast_to(value[:, index : index + 1], (SUB, LANES))


def own_columns(cols, turned, d):
    turned[...] = pltpu.roll(cols[...], lax.rem(LANES - d * SUB, LANES), axis=1)


def put(result, g, slot, value):
    rows = pl.ds(pl.multiple_of(g * SUB, SUB), SUB)
    total = jnp.sum(value, axis=1, keepdims=True)
    result[rows, :] = jnp.where(lane_iota() == slot, total, result[rows, :])


def far_row(ref, d, t, field):
    return jnp.broadcast_to(ref[d, t, field : field + 1, :], (SUB, LANES))


def distance(own, far):
    dx, dy, dz = own[0] - far[0], own[1] - far[1], own[2] - far[2]
    square = dx * dx + dy * dy + dz * dz
    return (dx, dy, dz), square * lax.rsqrt(jnp.maximum(square, TINY))


def density_body(groups, blocks, width, nbr, tiles, *refs):
    seg = refs[:groups]
    first, second = refs[groups : groups + 2]
    (vol_out, rho_out, far, cols, own_rows, index_out) = refs[groups + 2 : groups + 8]
    (region, aux, meta, table, inverse, own_tiles, turned, result, sem) = refs[groups + 8 :]
    slab = groups * blocks
    pairs = blocks // 2
    main = pairs * SUB
    me = lax.axis_index("seg")
    base_first, base_second = range_bases(slab)
    for k in range(groups):
        s = jnp.bitwise_xor(me, k)
        for base, tile in (
            (slab, seg[k][main : main + SUB, :]),
            (base_first, first[k * (main + SUB) + main : (k + 1) * (main + SUB), :]),
            (base_second, second[k * (main + SUB) + main : (k + 1) * (main + SUB), :]),
        ):
            rows = pl.ds(pl.multiple_of(base + s * blocks, SUB), SUB)
            meta[rows, :] = tile.astype(jnp.int32)
    copy = pltpu.make_async_copy(meta, table, sem)
    copy.start()
    for k in range(groups):
        s = jnp.bitwise_xor(me, k)
        for base, ref, start in (
            (slab, seg[k], 0),
            (base_first, first, k * (main + SUB)),
            (base_second, second, k * (main + SUB)),
        ):
            for p in range(pairs):
                even, odd = spread_tile(ref[start + p * SUB : start + (p + 1) * SUB, :], width)
                at = base + s * blocks + 2 * p
                region[at] = even
                region[at + 1] = odd
        aux[2 * s] = seg[k][main + SUB : main + 2 * SUB, :]
        aux[2 * s + 1] = seg[k][main + 2 * SUB : main + 3 * SUB, :]
    region[3 * slab] = jnp.zeros((SUB, LANES), jnp.float32)
    own_tiles[...] = jnp.zeros_like(own_tiles)
    result[...] = jnp.zeros_like(result)
    copy.wait()

    def invert(k, carry):
        inverse[table[slab + k, nbr]] = k
        return carry

    lax.fori_loop(0, slab, invert, 0)
    lane = lane_iota(1)

    def gather(d, carry):
        k = inverse[me * blocks + d]
        tile = region[slab + k]
        own_tiles[pl.ds(pl.multiple_of(d * SUB, SUB), SUB), :] = tile
        own_rows[pl.ds(d, SUB, stride=SUB), :] = tile
        s, b = k // blocks, lax.rem(k, blocks)
        p, half = b // 2, lax.rem(b, 2)
        for n, (at, r) in enumerate(((2 * s, p), (2 * s, pairs + p), (2 * s + 1, p))):
            value = aux[at, pl.ds(r, 1), :]
            other = pltpu.roll(value, width, axis=1)
            value = jnp.where(lane // width == half, value, other)
            own_rows[pl.ds((SUB + n) * SUB + d, 1), :] = value
        for t in range(tiles):
            pick = []
            for n in (2 * t, 2 * t + 1):
                if n == 0:
                    pick.append(slab + k)
                elif n <= nbr:
                    pick.append(table[slab + k, n - 1])
                else:
                    pick.append(3 * slab)
            far[d, t] = far_pair(region[pick[0]], region[pick[1]])
        return carry

    lax.fori_loop(0, blocks, gather, 0)
    cols[...] = jnp.transpose(own_tiles[...])[0:width, :]

    def slot(d, carry):
        own_columns(cols, turned, d)

        def group(g, carry):
            own = turned[pl.ds(pl.multiple_of(g * SUB, SUB), SUB), :]
            pos = [column(own, X + a) for a in range(3)]
            scale = 0.5 / column(own, SMOOTH)
            total = jnp.zeros((SUB, LANES), jnp.float32)
            for t in range(tiles):
                _, dist = distance(pos, [far_row(far, d, t, X + a) for a in range(3)])
                ratio = dist * scale
                shell = jnp.maximum(1.0 - ratio, 0.0)
                shell = shell * shell
                shell = shell * shell
                total += shell * (far_row(far, d, t, MASS) * (1.0 + 4.0 * ratio))
            put(result, g, d, total)
            return carry

        return lax.fori_loop(0, width // SUB, group, carry)

    lax.fori_loop(0, blocks, slot, 0)
    sums = jnp.transpose(result[...])[0:SUB, 0:width]
    smooth = own_rows[SMOOTH * SUB : (SMOOTH + 1) * SUB, 0:width]
    live = own_rows[10 * SUB : 11 * SUB, 0:width]
    rho = SIGMA / (smooth * smooth * smooth) * sums + (1.0 - live)
    rho_out[...] = rho
    vol = own_rows[MASS * SUB : (MASS + 1) * SUB, 0:width] / rho
    vol_out[...] = jnp.concatenate([vol, vol], axis=1)

    def remap(d, carry):
        k = inverse[me * blocks + d]
        for n in range(2 * tiles):
            if n == 0:
                j = slab + k
            elif n <= nbr:
                j = table[slab + k, n - 1]
            else:
                index_out[d, n] = 3 * slab
                continue
            start = jnp.where(j < slab, 0, jnp.where(j < 2 * slab, slab, 2 * slab))
            index_out[d, n] = start + table[j, nbr]
        return carry

    lax.fori_loop(0, blocks, remap, 0)


def factor_body(blocks, width, tiles, far, cols, out, turned):
    def slot(d, carry):
        own_columns(cols, turned, d)

        def group(g, carry):
            own = turned[pl.ds(pl.multiple_of(g * SUB, SUB), SUB), :]
            pos = [column(own, X + a) for a in range(3)]
            smooth = column(own, SMOOTH)
            for t in range(tiles):
                _, dist = distance(pos, [far_row(far, d, t, X + a) for a in range(3)])
                inv = 1.0 / (smooth + far_row(far, d, t, SMOOTH))
                inv2 = inv * inv
                part = jnp.maximum(inv - dist * inv2, 0.0)
                out[d, g, t] = part * part * part * inv2
            return carry

        return lax.fori_loop(0, width // SUB, group, carry)

    lax.fori_loop(0, blocks, slot, 0)


def place_region(groups, blocks, refs, store):
    slab = groups * blocks
    me = lax.axis_index("seg")
    base_first, base_second = range_bases(slab)
    size = refs[0].shape[0]
    for k in range(groups):
        s = jnp.bitwise_xor(me, k)
        for base, ref, start in (
            (slab, refs[k], 0),
            (base_first, refs[groups], k * size),
            (base_second, refs[groups + 1], k * size),
        ):
            store(pl.multiple_of(base + s * blocks, SUB), ref, start)


def tensor_body(groups, blocks, width, tiles, *refs):
    index = refs[0]
    far, cols, own_rows, factor, rho = refs[1:6]
    vols = refs[6 : 6 + groups + 2]
    coef_out, corr_out = refs[8 + groups : 10 + groups]
    turned, region, far_vol, result = refs[10 + groups :]
    slab = groups * blocks

    def store(at, ref, start):
        region[pl.ds(at, SUB), :] = ref[start : start + SUB, :]

    place_region(groups, blocks, vols, store)
    region[3 * slab : 3 * slab + SUB, :] = jnp.zeros((SUB, LANES), jnp.float32)
    result[...] = jnp.zeros_like(result)

    def slot(d, carry):
        own_columns(cols, turned, d)
        for t in range(tiles):
            left = region[pl.ds(index[d, 2 * t], 1), :]
            right = region[pl.ds(index[d, 2 * t + 1], 1), :]
            far_vol[t] = jnp.broadcast_to(far_pair(left, right), (SUB, LANES))

        def group(g, carry):
            own = turned[pl.ds(pl.multiple_of(g * SUB, SUB), SUB), :]
            pos = [column(own, X + a) for a in range(3)]
            total = [jnp.zeros((SUB, LANES), jnp.float32) for _ in range(6)]
            for t in range(tiles):
                dx, dy, dz = [pos[a] - far_row(far, d, t, X + a) for a in range(3)]
                weight = factor[d, g, t] * far_vol[t]
                wx, wy, wz = weight * dx, weight * dy, weight * dz
                for n, term in enumerate((wx * dx, wy * dy, wz * dz, wx * dy, wx * dz, wy * dz)):
                    total[n] += term
            for n in range(6):
                put(result, g, n * blocks + d, total[n])
            return carry

        return lax.fori_loop(0, width // SUB, group, carry)

    lax.fori_loop(0, blocks, slot, 0)
    sums = jnp.transpose(result[...])
    press = GAMMA_LESS * own_rows[SUB * SUB : 9 * SUB, 0:width] / rho[...]
    scale = own_rows[MASS * SUB : (MASS + 1) * SUB, 0:width] * press
    coefs = []
    for n in range(6):
        tensor = SLOPE * sums[n * blocks : (n + 1) * blocks, 0:width]
        corr = (2.0 + tensor) if n < 3 else tensor
        corr_out[n] = corr
        coefs.append(scale * corr)
    corr_out[6] = press
    for n in range(3):
        coef_out[n * SUB : (n + 1) * SUB, :] = jnp.concatenate([coefs[n], coefs[n + 3]], axis=1)


def moment_body(blocks, width, tiles, far, cols, factor, out, turned, result):
    result[...] = jnp.zeros_like(result)

    def slot(d, carry):
        own_columns(cols, turned, d)

        def group(g, carry):
            own = turned[pl.ds(pl.multiple_of(g * SUB, SUB), SUB), :]
            pos = [column(own, X + a) for a in range(3)]
            vel = [column(own, VEL + a) for a in range(3)]
            total = [jnp.zeros((SUB, LANES), jnp.float32) for _ in range(9)]
            for t in range(tiles):
                weight = factor[d, g, t] * far_row(far, d, t, MASS)
                px, py, pz = [weight * (pos[a] - far_row(far, d, t, X + a)) for a in range(3)]
                vx, vy, vz = [vel[a] - far_row(far, d, t, VEL + a) for a in range(3)]
                terms = (
                    px,
                    py,
                    pz,
                    vx * px,
                    vy * py,
                    vz * pz,
                    vx * py + vy * px,
                    vx * pz + vz * px,
                    vy * pz + vz * py,
                )
                for n, term in enumerate(terms):
                    total[n] += term
            for n in range(9):
                put(result, g, n * blocks + d, total[n])
            return carry

        return lax.fori_loop(0, width // SUB, group, carry)

    lax.fori_loop(0, blocks, slot, 0)
    sums = jnp.transpose(result[...])
    for n in range(9):
        out[n] = sums[n * blocks : (n + 1) * blocks, 0:width]


def update_body(groups, blocks, width, tiles, *refs):
    index = refs[0]
    far, cols, own_rows, factor, corr, moments = refs[1:7]
    coefs = refs[7 : 9 + groups]
    state_out = refs[9 + groups]
    turned, region, far_coef, result = refs[10 + groups :]
    slab = groups * blocks

    def store(at, ref, start):
        for n in range(3):
            low, high = spread_tile(ref[start + n * SUB : start + (n + 1) * SUB, :], width)
            region[n, pl.ds(at, SUB), :] = low
            region[n + 3, pl.ds(at, SUB), :] = high

    place_region(groups, blocks, coefs, store)
    for n in range(6):
        region[n, 3 * slab : 3 * slab + SUB, :] = jnp.zeros((SUB, LANES), jnp.float32)
    result[...] = jnp.zeros_like(result)

    def slot(d, carry):
        own_columns(cols, turned, d)
        for t in range(tiles):
            one, two = index[d, 2 * t], index[d, 2 * t + 1]
            for n in range(6):
                value = far_pair(region[n, pl.ds(one, 1), :], region[n, pl.ds(two, 1), :])
                far_coef[t, n] = jnp.broadcast_to(value, (SUB, LANES))

        def group(g, carry):
            own = turned[pl.ds(pl.multiple_of(g * SUB, SUB), SUB), :]
            pos = [column(own, X + a) for a in range(3)]
            total = [jnp.zeros((SUB, LANES), jnp.float32) for _ in range(3)]
            for t in range(tiles):
                weight = factor[d, g, t]
                ex, ey, ez = [weight * (pos[a] - far_row(far, d, t, X + a)) for a in range(3)]
                xx, yy, zz, xy, xz, yz = [far_coef[t, n] for n in range(6)]
                total[0] += xx * ex + xy * ey + xz * ez
                total[1] += xy * ex + yy * ey + yz * ez
                total[2] += xz * ex + yz * ey + zz * ez
            for n in range(3):
                put(result, g, n * blocks + d, total[n])
            return carry

        return lax.fori_loop(0, width // SUB, group, carry)

    lax.fori_loop(0, blocks, slot, 0)
    sums = jnp.transpose(result[...])
    field = lambda n: own_rows[n * SUB : (n + 1) * SUB, 0:width]
    live, press = field(10), corr[6]
    xx, yy, zz, xy, xz, yz = [corr[n] for n in range(6)]
    sx, sy, sz = [moments[n] for n in range(3)]
    near = (xx * sx + xy * sy + xz * sz, xy * sx + yy * sy + yz * sz, xz * sx + yz * sy + zz * sz)
    outs = {}
    for a in range(3):
        far_sum = sums[a * blocks : (a + 1) * blocks, 0:width]
        accel = -SLOPE * live * (press * near[a] + far_sum)
        velocity = field(VEL + a) + STEP_DT * accel
        outs[VEL + a] = velocity
        outs[X + a] = field(X + a) + STEP_DT * velocity
    heat = moments[3] * xx + moments[4] * yy + moments[5] * zz
    heat += moments[6] * xy + moments[7] * xz + moments[8] * yz
    outs[MASS] = field(9)
    outs[SMOOTH] = field(SMOOTH)
    outs[8] = field(8) + STEP_DT * (SLOPE * live * press * heat)
    for n in range(9):
        state_out[:, n, :] = outs[n]


def exchange(own, send_rows):
    groups = lax.axis_size("seg")
    ranges = lax.axis_size("dom")
    seg = [own]
    for k in range(1, groups):
        seg.append(lax.ppermute(own, "seg", [(i, i ^ k) for i in range(groups)]))
    whole = jnp.concatenate([part[:send_rows] for part in seg], axis=0)
    first = [(i, i ^ 1) for i in range(ranges)]
    second = [(i, ((i + 1) ^ 1) - 1) for i in range(1, ranges - 1)]
    return seg + [lax.ppermute(whole, "dom", first), lax.ppermute(whole, "dom", second)]


def local(state, counts, neighbours, new_place):
    blocks, fields, width = state.shape
    nbr = neighbours.shape[1]
    groups = lax.axis_size("seg")
    slab = blocks * groups
    pairs = blocks // 2
    tiles = (nbr + 2) // 2
    main = pairs * SUB
    f32, i32 = jnp.float32, jnp.int32
    vm = pl.BlockSpec(memory_space=VMEM)
    sm = pl.BlockSpec(memory_space=SMEM)
    packed = call(
        functools.partial(pack_body, blocks, width, nbr),
        shape(main + 3 * SUB, LANES),
        in_specs=[sm, sm, vm, vm],
        out_specs=vm,
        name="pack",
    )(counts, new_place, state, neighbours)
    parts = exchange(packed, main + SUB)
    vol, rho, far, cols, own_rows, index = call(
        functools.partial(density_body, groups, blocks, width, nbr, tiles),
        (
            shape(SUB, LANES),
            shape(blocks, width),
            shape(blocks, tiles, SUB, LANES),
            shape(width, LANES),
            shape(11 * SUB, LANES),
            shape(blocks, 2 * tiles, dtype=i32),
        ),
        in_specs=[vm] * (groups + 2),
        out_specs=(vm, vm, vm, vm, vm, sm),
        scratch=(
            VMEM((3 * slab + 1, SUB, LANES), f32),
            VMEM((2 * groups, SUB, LANES), f32),
            VMEM((3 * slab, LANES), i32),
            SMEM((3 * slab, LANES), i32),
            SMEM((slab,), i32),
            VMEM((LANES, LANES), f32),
            VMEM((width, LANES), f32),
            VMEM((width, LANES), f32),
            pltpu.SemaphoreType.DMA,
        ),
        name="density",
    )(*parts)
    vols = exchange(vol, SUB)
    factor = call(
        functools.partial(factor_body, blocks, width, tiles),
        shape(blocks, width // SUB, tiles, SUB, LANES),
        in_specs=[vm, vm],
        out_specs=vm,
        scratch=(VMEM((width, LANES), f32),),
        name="factor",
    )(far, cols)
    coef, corr = call(
        functools.partial(tensor_body, groups, blocks, width, tiles),
        (shape(3 * SUB, LANES), shape(7, blocks, width)),
        in_specs=[sm] + [vm] * (5 + groups + 2),
        out_specs=(vm, vm),
        scratch=(
            VMEM((width, LANES), f32),
            VMEM((3 * slab + SUB, LANES), f32),
            VMEM((tiles, SUB, LANES), f32),
            VMEM((width, LANES), f32),
        ),
        name="tensor",
    )(index, far, cols, own_rows, factor, rho, *vols)
    coefs = exchange(coef, 3 * SUB)
    moments = call(
        functools.partial(moment_body, blocks, width, tiles),
        shape(9, blocks, width),
        in_specs=[vm] * 3,
        out_specs=vm,
        scratch=(VMEM((width, LANES), f32), VMEM((width, LANES), f32)),
        name="moments",
    )(far, cols, factor)
    moved = call(
        functools.partial(update_body, groups, blocks, width, tiles),
        shape(blocks, fields, width),
        in_specs=[sm] + [vm] * (6 + groups + 2),
        out_specs=vm,
        scratch=(
            VMEM((width, LANES), f32),
            VMEM((6, 3 * slab + SUB, LANES), f32),
            VMEM((tiles, 6, SUB, LANES), f32),
            VMEM((width, LANES), f32),
        ),
        name="update",
    )(index, far, cols, own_rows, factor, corr, moments, *coefs)
    return (moved, rho)


def solution(mesh):
    return jax.shard_map(
        local,
        mesh=mesh,
        in_specs=(
            P(("dom", "seg"), None, None),
            P(("dom", "seg")),
            P(("dom", "seg"), None),
            P(("dom", "seg")),
        ),
        out_specs=(P(("dom", "seg"), None, None), P(("dom", "seg"), None)),
        check_vma=False,
    )
```

```python
import functools
import math

import jax
import jax.numpy as jnp
from jax import lax
from jax.experimental import pallas as pl
from jax.experimental.pallas import tpu as pltpu
from jax.sharding import PartitionSpec as P

SIGMA = 21.0 / (16.0 * math.pi)
GAMMA_LESS = 2.0 / 3.0
STEP_DT = 0.1
SLOPE = -5.0 * SIGMA * 32.0
TINY = 1e-37
UNROLL = (8, 8, 8, 8, 8)
GRANT = (4, 4, 4, 4, 4, 4)
SUB = 8
LANES = 128
X, VEL, MASS, SMOOTH = 0, 3, 6, 7
VMEM = pltpu.VMEM
SMEM = pltpu.SMEM


def lane_iota(rows=SUB):
    return lax.broadcasted_iota(jnp.int32, (rows, LANES), 1)


def row_iota(rows=SUB):
    return lax.broadcasted_iota(jnp.int32, (rows, LANES), 0)


def call(body, outs, scratch=(), in_specs=None, out_specs=None, name=None, grant=8):
    return pl.pallas_call(
        body,
        out_shape=outs,
        in_specs=in_specs,
        out_specs=out_specs,
        scratch_shapes=list(scratch),
        compiler_params=pltpu.CompilerParams(vmem_limit_bytes=grant << 20),
        name=name,
    )


def shape(*dims, dtype=jnp.float32):
    return jax.ShapeDtypeStruct(dims, dtype)


def pack_body(blocks, width, nbr, fields, counts, place, state, lists, out):
    pairs = blocks // 2
    lane = lane_iota()
    row = row_iota()
    low = lane < width
    meta = jnp.concatenate(
        [lists[...].astype(jnp.float32), jnp.zeros((blocks, LANES - nbr), jnp.float32)], axis=1
    )
    for b in range(blocks):
        meta = jnp.where((row == b) & (lane == nbr), place[b].astype(jnp.float32), meta)
    base = pairs * SUB
    out[base : base + SUB, :] = meta
    for p in range(pairs):
        even, odd = [state[pl.ds(2 * p + n, SUB, stride=SUB), :] for n in (0, 1)]
        tile = jnp.concatenate([even, odd], axis=1)
        at = 8 * SUB + 2 * p
        energy = jnp.concatenate([state[at : at + 1, :], state[at + 1 : at + 2, :]], axis=1)
        live = lane < jnp.where(low, counts[2 * p], counts[2 * p + 1] + width)
        out[p * SUB : (p + 1) * SUB, :] = jnp.where((row == MASS) & jnp.logical_not(live), 0.0, tile)
        out[base + SUB + p : base + SUB + p + 1, :] = energy
        out[base + SUB + pairs + p : base + SUB + pairs + p + 1, :] = tile[MASS : MASS + 1]
        out[base + 2 * SUB + p : base + 2 * SUB + p + 1, :] = jnp.where(live, 1.0, 0.0)[0:1]
    out[base + 2 * SUB + pairs : base + 3 * SUB, :] = jnp.zeros((SUB - pairs, LANES), jnp.float32)


def range_bases(slab):
    odd = lax.rem(lax.axis_index("dom"), 2)
    first = jnp.where(odd == 0, 2 * slab, 0)
    second = jnp.where(odd == 0, 0, 2 * slab)
    return first, second


def spread_tile(tile, width):
    low = lane_iota(tile.shape[0]) < width
    turned = pltpu.roll(tile, width, axis=1)
    return jnp.where(low, tile, turned), jnp.where(low, turned, tile)


def far_pair(left, right):
    return jnp.where(lane_iota(left.shape[0]) < LANES // 2, left, right)


def column(value, index):
    return jnp.broadcast_to(value[:, index : index + 1], (SUB, LANES))


def own_columns(cols, turned, d):
    turned[...] = pltpu.roll(cols[...], lax.rem(LANES - d * SUB, LANES), axis=1)


def each_group(width, unroll, group):
    count = width // SUB

    def step(i, carry):
        for n in range(unroll):
            group(i * unroll + n)
        return carry

    if unroll == count:
        step(0, 0)
    else:
        lax.fori_loop(0, count // unroll, step, 0)


def group_rows(g):
    return pl.ds(g * SUB if isinstance(g, int) else pl.multiple_of(g * SUB, SUB), SUB)


def put(result, g, slot, value):
    rows = group_rows(g)
    total = jnp.sum(value, axis=1, keepdims=True)
    result[rows, :] = jnp.where(lane_iota() == slot, total, result[rows, :])


def far_row(ref, d, t, field):
    return jnp.broadcast_to(ref[d, t, field : field + 1, :], (SUB, LANES))


def distance(own, far):
    dx, dy, dz = own[0] - far[0], own[1] - far[1], own[2] - far[2]
    square = dx * dx + dy * dy + dz * dz
    return (dx, dy, dz), square * lax.rsqrt(jnp.maximum(square, TINY))


def invert(inverse, table, slab, nbr):
    for k in range(slab):
        inverse[table[slab + k, nbr]] = k


def density_body(groups, blocks, width, nbr, tiles, *refs):
    seg = refs[:groups]
    first, second = refs[groups : groups + 2]
    (vol_out, rho_out, far, cols, own_rows, meta) = refs[groups + 2 : groups + 8]
    (region, aux, table, inverse, own_tiles, turned, result, sem) = refs[groups + 8 :]
    slab = groups * blocks
    pairs = blocks // 2
    main = pairs * SUB
    me = lax.axis_index("seg")
    base_first, base_second = range_bases(slab)
    for k in range(groups):
        s = jnp.bitwise_xor(me, k)
        for base, tile in (
            (slab, seg[k][main : main + SUB, :]),
            (base_first, first[k * (main + SUB) + main : (k + 1) * (main + SUB), :]),
            (base_second, second[k * (main + SUB) + main : (k + 1) * (main + SUB), :]),
        ):
            rows = pl.ds(pl.multiple_of(base + s * blocks, SUB), SUB)
            meta[rows, :] = tile.astype(jnp.int32)
    copy = pltpu.make_async_copy(meta, table, sem)
    copy.start()
    for k in range(groups):
        s = jnp.bitwise_xor(me, k)
        for base, ref, start in (
            (slab, seg[k], 0),
            (base_first, first, k * (main + SUB)),
            (base_second, second, k * (main + SUB)),
        ):
            for p in range(pairs):
                even, odd = spread_tile(ref[start + p * SUB : start + (p + 1) * SUB, :], width)
                at = base + s * blocks + 2 * p
                region[at] = even
                region[at + 1] = odd
        aux[2 * s] = seg[k][main + SUB : main + 2 * SUB, :]
        aux[2 * s + 1] = seg[k][main + 2 * SUB : main + 3 * SUB, :]
    region[3 * slab] = jnp.zeros((SUB, LANES), jnp.float32)
    own_tiles[...] = jnp.zeros_like(own_tiles)
    result[...] = jnp.zeros_like(result)
    copy.wait()

    invert(inverse, table, slab, nbr)
    lane = lane_iota(1)

    def gather(d, carry):
        k = inverse[me * blocks + d]
        tile = region[slab + k]
        own_tiles[pl.ds(pl.multiple_of(d * SUB, SUB), SUB), :] = tile
        own_rows[pl.ds(d, SUB, stride=SUB), :] = tile
        s, b = k // blocks, lax.rem(k, blocks)
        p, half = b // 2, lax.rem(b, 2)
        for n, (at, r) in enumerate(((2 * s, p), (2 * s, pairs + p), (2 * s + 1, p))):
            value = aux[at, pl.ds(r, 1), :]
            other = pltpu.roll(value, width, axis=1)
            value = jnp.where(lane // width == half, value, other)
            own_rows[pl.ds((SUB + n) * SUB + d, 1), :] = value
        for t in range(tiles):
            pick = []
            for n in (2 * t, 2 * t + 1):
                if n == 0:
                    pick.append(slab + k)
                elif n <= nbr:
                    pick.append(table[slab + k, n - 1])
                else:
                    pick.append(3 * slab)
            far[d, t] = far_pair(region[pick[0]], region[pick[1]])
        return carry

    lax.fori_loop(0, blocks, gather, 0)
    cols[...] = jnp.transpose(own_tiles[...])[0:width, :]

    def slot(d, carry):
        own_columns(cols, turned, d)

        def group(g):
            own = turned[group_rows(g), :]
            pos = [column(own, X + a) for a in range(3)]
            scale = 0.5 / column(own, SMOOTH)
            total = jnp.zeros((SUB, LANES), jnp.float32)
            for t in range(tiles):
                _, dist = distance(pos, [far_row(far, d, t, X + a) for a in range(3)])
                ratio = dist * scale
                shell = jnp.maximum(1.0 - ratio, 0.0)
                shell = shell * shell
                shell = shell * shell
                total += shell * (far_row(far, d, t, MASS) * (0.25 + ratio))
            put(result, g, d, total)

        each_group(width, UNROLL[0], group)
        return carry

    lax.fori_loop(0, blocks, slot, 0)
    sums = jnp.transpose(result[...])[0:SUB, 0:width]
    smooth = own_rows[SMOOTH * SUB : (SMOOTH + 1) * SUB, 0:width]
    live = own_rows[10 * SUB : 11 * SUB, 0:width]
    rho = 4.0 * SIGMA / (smooth * smooth * smooth) * sums + (1.0 - live)
    rho_out[...] = rho
    vol = own_rows[MASS * SUB : (MASS + 1) * SUB, 0:width] / rho
    vol_out[...] = jnp.concatenate([vol, vol], axis=1)


def factor_body(groups, blocks, width, nbr, tiles, *refs):
    far, cols, meta, out, index_out, turned, table, inverse, sem = refs
    slab = groups * blocks
    me = lax.axis_index("seg")
    copy = pltpu.make_async_copy(meta, table, sem)
    copy.start()

    def slot(d, carry):
        own_columns(cols, turned, d)

        def group(g):
            own = turned[group_rows(g), :]
            pos = [column(own, X + a) for a in range(3)]
            smooth = column(own, SMOOTH)
            for t in range(tiles):
                _, dist = distance(pos, [far_row(far, d, t, X + a) for a in range(3)])
                inv = 1.0 / (smooth + far_row(far, d, t, SMOOTH))
                inv2 = inv * inv
                part = jnp.maximum(inv - dist * inv2, 0.0)
                out[d, g, t] = part * part * part * inv2

        each_group(width, UNROLL[1], group)
        return carry

    lax.fori_loop(0, blocks, slot, 0)
    copy.wait()
    invert(inverse, table, slab, nbr)

    def remap(d, carry):
        k = inverse[me * blocks + d]
        for n in range(2 * tiles):
            if n > nbr:
                index_out[d, n] = 3 * slab
                continue
            j = slab + k if n == 0 else table[slab + k, n - 1]
            start = jnp.where(j < slab, 0, jnp.where(j < 2 * slab, slab, 2 * slab))
            index_out[d, n] = start + table[j, nbr]
        return carry

    lax.fori_loop(0, blocks, remap, 0)


def place_region(groups, blocks, refs, store):
    slab = groups * blocks
    me = lax.axis_index("seg")
    base_first, base_second = range_bases(slab)
    size = refs[0].shape[0]
    for k in range(groups):
        s = jnp.bitwise_xor(me, k)
        for base, ref, start in (
            (slab, refs[k], 0),
            (base_first, refs[groups], k * size),
            (base_second, refs[groups + 1], k * size),
        ):
            store(pl.multiple_of(base + s * blocks, SUB), ref, start)


def tensor_body(groups, blocks, width, tiles, *refs):
    index = refs[0]
    far, cols, own_rows, factor, rho = refs[1:6]
    vols = refs[6 : 6 + groups + 2]
    coef_out, corr_out = refs[8 + groups : 10 + groups]
    turned, region, far_vol, result = refs[10 + groups :]
    slab = groups * blocks

    def store(at, ref, start):
        region[pl.ds(at, SUB), :] = ref[start : start + SUB, :]

    place_region(groups, blocks, vols, store)
    region[3 * slab : 3 * slab + SUB, :] = jnp.zeros((SUB, LANES), jnp.float32)
    result[...] = jnp.zeros_like(result)

    def slot(d, carry):
        own_columns(cols, turned, d)
        for t in range(tiles):
            left = region[pl.ds(index[d, 2 * t], 1), :]
            right = region[pl.ds(index[d, 2 * t + 1], 1), :]
            far_vol[t] = jnp.broadcast_to(far_pair(left, right), (SUB, LANES))

        def group(g):
            own = turned[group_rows(g), :]
            pos = [column(own, X + a) for a in range(3)]
            total = [jnp.zeros((SUB, LANES), jnp.float32) for _ in range(6)]
            for t in range(tiles):
                dx, dy, dz = [pos[a] - far_row(far, d, t, X + a) for a in range(3)]
                weight = factor[d, g, t] * far_vol[t]
                wx, wy, wz = weight * dx, weight * dy, weight * dz
                for n, term in enumerate((wx * dx, wy * dy, wz * dz, wx * dy, wx * dz, wy * dz)):
                    total[n] += term
            for n in range(6):
                put(result, g, n * blocks + d, total[n])

        each_group(width, UNROLL[2], group)
        return carry

    lax.fori_loop(0, blocks, slot, 0)
    sums = jnp.transpose(result[...])
    press = GAMMA_LESS * own_rows[SUB * SUB : 9 * SUB, 0:width] / rho[...]
    scale = own_rows[MASS * SUB : (MASS + 1) * SUB, 0:width] * press
    coefs = []
    for n in range(6):
        tensor = SLOPE * sums[n * blocks : (n + 1) * blocks, 0:width]
        corr = (2.0 + tensor) if n < 3 else tensor
        corr_out[n] = corr
        coefs.append(scale * corr)
    corr_out[6] = press
    for n in range(3):
        coef_out[n * SUB : (n + 1) * SUB, :] = jnp.concatenate([coefs[n], coefs[n + 3]], axis=1)


def moment_body(blocks, width, tiles, far, cols, factor, out, turned, result):
    result[...] = jnp.zeros_like(result)

    def slot(d, carry):
        own_columns(cols, turned, d)

        def group(g):
            own = turned[group_rows(g), :]
            pos = [column(own, X + a) for a in range(3)]
            vel = [column(own, VEL + a) for a in range(3)]
            total = [jnp.zeros((SUB, LANES), jnp.float32) for _ in range(9)]
            for t in range(tiles):
                weight = factor[d, g, t] * far_row(far, d, t, MASS)
                px, py, pz = [weight * (pos[a] - far_row(far, d, t, X + a)) for a in range(3)]
                vx, vy, vz = [vel[a] - far_row(far, d, t, VEL + a) for a in range(3)]
                terms = (
                    px,
                    py,
                    pz,
                    vx * px,
                    vy * py,
                    vz * pz,
                    vx * py + vy * px,
                    vx * pz + vz * px,
                    vy * pz + vz * py,
                )
                for n, term in enumerate(terms):
                    total[n] += term
            for n in range(9):
                put(result, g, n * blocks + d, total[n])

        each_group(width, UNROLL[3], group)
        return carry

    lax.fori_loop(0, blocks, slot, 0)
    sums = jnp.transpose(result[...])
    for n in range(9):
        out[n] = sums[n * blocks : (n + 1) * blocks, 0:width]


def update_body(groups, blocks, width, tiles, *refs):
    index = refs[0]
    far, cols, own_rows, factor, corr, moments = refs[1:7]
    coefs = refs[7 : 9 + groups]
    state_out = refs[9 + groups]
    turned, region, far_coef, result = refs[10 + groups :]
    slab = groups * blocks

    def store(at, ref, start):
        for n in range(3):
            low, high = spread_tile(ref[start + n * SUB : start + (n + 1) * SUB, :], width)
            region[n, pl.ds(at, SUB), :] = low
            region[n + 3, pl.ds(at, SUB), :] = high

    place_region(groups, blocks, coefs, store)
    for n in range(6):
        region[n, 3 * slab : 3 * slab + SUB, :] = jnp.zeros((SUB, LANES), jnp.float32)
    result[...] = jnp.zeros_like(result)

    def slot(d, carry):
        own_columns(cols, turned, d)
        for t in range(tiles):
            one, two = index[d, 2 * t], index[d, 2 * t + 1]
            for n in range(6):
                value = far_pair(region[n, pl.ds(one, 1), :], region[n, pl.ds(two, 1), :])
                far_coef[t, n] = jnp.broadcast_to(value, (SUB, LANES))

        def group(g):
            own = turned[group_rows(g), :]
            pos = [column(own, X + a) for a in range(3)]
            total = [jnp.zeros((SUB, LANES), jnp.float32) for _ in range(3)]
            for t in range(tiles):
                weight = factor[d, g, t]
                ex, ey, ez = [weight * (pos[a] - far_row(far, d, t, X + a)) for a in range(3)]
                xx, yy, zz, xy, xz, yz = [far_coef[t, n] for n in range(6)]
                total[0] += xx * ex + xy * ey + xz * ez
                total[1] += xy * ex + yy * ey + yz * ez
                total[2] += xz * ex + yz * ey + zz * ez
            for n in range(3):
                put(result, g, n * blocks + d, total[n])

        each_group(width, UNROLL[4], group)
        return carry

    lax.fori_loop(0, blocks, slot, 0)
    sums = jnp.transpose(result[...])
    field = lambda n: own_rows[n * SUB : (n + 1) * SUB, 0:width]
    live, press = field(10), corr[6]
    xx, yy, zz, xy, xz, yz = [corr[n] for n in range(6)]
    sx, sy, sz = [moments[n] for n in range(3)]
    near = (xx * sx + xy * sy + xz * sz, xy * sx + yy * sy + yz * sz, xz * sx + yz * sy + zz * sz)
    outs = {}
    for a in range(3):
        far_sum = sums[a * blocks : (a + 1) * blocks, 0:width]
        accel = -SLOPE * live * (press * near[a] + far_sum)
        velocity = field(VEL + a) + STEP_DT * accel
        outs[VEL + a] = velocity
        outs[X + a] = field(X + a) + STEP_DT * velocity
    heat = moments[3] * xx + moments[4] * yy + moments[5] * zz
    heat += moments[6] * xy + moments[7] * xz + moments[8] * yz
    outs[MASS] = field(9)
    outs[SMOOTH] = field(SMOOTH)
    outs[8] = field(8) + STEP_DT * (SLOPE * live * press * heat)
    for n in range(9):
        state_out[n] = outs[n]


def exchange(own, send_rows):
    groups = lax.axis_size("seg")
    ranges = lax.axis_size("dom")
    seg = [own]
    for k in range(1, groups):
        seg.append(lax.ppermute(own, "seg", [(i, i ^ k) for i in range(groups)]))
    whole = jnp.concatenate([part[:send_rows] for part in seg], axis=0)
    first = [(i, i ^ 1) for i in range(ranges)]
    second = [(i, ((i + 1) ^ 1) - 1) for i in range(1, ranges - 1)]
    return seg + [lax.ppermute(whole, "dom", first), lax.ppermute(whole, "dom", second)]


def local(state, counts, neighbours, new_place):
    blocks, fields, width = state.shape
    nbr = neighbours.shape[1]
    groups = lax.axis_size("seg")
    slab = blocks * groups
    pairs = blocks // 2
    tiles = (nbr + 2) // 2
    main = pairs * SUB
    f32, i32 = jnp.float32, jnp.int32
    vm = pl.BlockSpec(memory_space=VMEM)
    sm = pl.BlockSpec(memory_space=SMEM)
    packed = call(
        functools.partial(pack_body, blocks, width, nbr, fields),
        shape(main + 3 * SUB, LANES),
        in_specs=[sm, sm, vm, vm],
        out_specs=vm,
        name="pack",
    )(counts, new_place, jnp.swapaxes(state, 0, 1).reshape(fields * blocks, width), neighbours)
    parts = exchange(packed, main + SUB)
    vol, rho, far, cols, own_rows, meta = call(
        functools.partial(density_body, groups, blocks, width, nbr, tiles),
        (
            shape(SUB, LANES),
            shape(blocks, width),
            shape(blocks, tiles, SUB, LANES),
            shape(width, LANES),
            shape(11 * SUB, LANES),
            shape(3 * slab, LANES, dtype=i32),
        ),
        in_specs=[vm] * (groups + 2),
        out_specs=(vm,) * 6,
        scratch=(
            VMEM((3 * slab + 1, SUB, LANES), f32),
            VMEM((2 * groups, SUB, LANES), f32),
            SMEM((3 * slab, LANES), i32),
            SMEM((slab,), i32),
            VMEM((LANES, LANES), f32),
            VMEM((width, LANES), f32),
            VMEM((width, LANES), f32),
            pltpu.SemaphoreType.DMA,
        ),
        name="density",
    )(*parts)
    vols = exchange(vol, SUB)
    factor, index = call(
        functools.partial(factor_body, groups, blocks, width, nbr, tiles),
        (shape(blocks, width // SUB, tiles, SUB, LANES), shape(blocks, 2 * tiles, dtype=i32)),
        in_specs=[vm, vm, vm],
        out_specs=(vm, sm),
        scratch=(
            VMEM((width, LANES), f32),
            SMEM((3 * slab, LANES), i32),
            SMEM((slab,), i32),
            pltpu.SemaphoreType.DMA,
        ),
        name="factor",
    )(far, cols, meta)
    coef, corr = call(
        functools.partial(tensor_body, groups, blocks, width, tiles),
        (shape(3 * SUB, LANES), shape(7, blocks, width)),
        in_specs=[sm] + [vm] * (5 + groups + 2),
        out_specs=(vm, vm),
        scratch=(
            VMEM((width, LANES), f32),
            VMEM((3 * slab + SUB, LANES), f32),
            VMEM((tiles, SUB, LANES), f32),
            VMEM((width, LANES), f32),
        ),
        name="tensor",
    )(index, far, cols, own_rows, factor, rho, *vols)
    coefs = exchange(coef, 3 * SUB)
    moments = call(
        functools.partial(moment_body, blocks, width, tiles),
        shape(9, blocks, width),
        in_specs=[vm] * 3,
        out_specs=vm,
        scratch=(VMEM((width, LANES), f32), VMEM((width, LANES), f32)),
        name="moments",
    )(far, cols, factor)
    moved = call(
        functools.partial(update_body, groups, blocks, width, tiles),
        shape(fields, blocks, width),
        in_specs=[sm] + [vm] * (6 + groups + 2),
        out_specs=vm,
        scratch=(
            VMEM((width, LANES), f32),
            VMEM((6, 3 * slab + SUB, LANES), f32),
            VMEM((tiles, 6, SUB, LANES), f32),
            VMEM((width, LANES), f32),
        ),
        name="update",
    )(index, far, cols, own_rows, factor, corr, moments, *coefs)
    return (jnp.swapaxes(moved, 0, 1), rho)


def solution(mesh):
    return jax.shard_map(
        local,
        mesh=mesh,
        in_specs=(
            P(("dom", "seg"), None, None),
            P(("dom", "seg")),
            P(("dom", "seg"), None),
            P(("dom", "seg")),
        ),
        out_specs=(P(("dom", "seg"), None, None), P(("dom", "seg"), None)),
        check_vma=False,
    )
```

```python
import functools
import math

import jax
import jax.numpy as jnp
from jax import lax
from jax.experimental import pallas as pl
from jax.experimental.pallas import tpu as pltpu
from jax.sharding import PartitionSpec as P

SIGMA = 21.0 / (16.0 * math.pi)
GAMMA_LESS = 2.0 / 3.0
STEP_DT = 0.1
SLOPE = -5.0 * SIGMA * 32.0
TINY = 1e-37
SUB = 8
LANES = 128
X, SMOOTH, MASS, VEL = 0, 3, 4, 5
HALF = LANES // 2
VMEM = pltpu.VMEM
SMEM = pltpu.SMEM


def lane_iota(rows=SUB):
    return lax.broadcasted_iota(jnp.int32, (rows, LANES), 1)


def row_iota(rows=SUB):
    return lax.broadcasted_iota(jnp.int32, (rows, LANES), 0)


def call(body, outs, scratch=(), in_specs=None, out_specs=None, name=None, grant=8):
    return pl.pallas_call(
        body,
        out_shape=outs,
        in_specs=in_specs,
        out_specs=out_specs,
        scratch_shapes=list(scratch),
        compiler_params=pltpu.CompilerParams(vmem_limit_bytes=grant << 20),
        name=name,
    )


def shape(*dims, dtype=jnp.float32):
    return jax.ShapeDtypeStruct(dims, dtype)


def pack_body(blocks, width, nbr, tiles, *refs):
    counts, place, state, lists, out, held, entries, few, ids, sem = refs
    copies = [
        pltpu.make_async_copy(source, target, sem.at[n])
        for n, (source, target) in enumerate(
            ((state, held), (lists, entries), (counts, few), (place, ids))
        )
    ]
    for copy in copies:
        copy.start()
    for copy in copies:
        copy.wait()
    groups = lax.axis_size("seg")
    me = lax.axis_index("seg")
    lane, row = lane_iota(), row_iota()
    count = jnp.zeros((SUB, LANES), jnp.int32)
    spot = jnp.zeros((SUB, LANES), jnp.int32)
    for b in range(blocks):
        count = jnp.where(row == b, few[b], count)
        spot = jnp.where(row == b, ids[b], spot)
    listed = jnp.concatenate(
        [entries[...], jnp.zeros((blocks, LANES - nbr), jnp.int32)], axis=1
    ).astype(jnp.float32)
    listed = pltpu.roll(listed, 1, axis=1)
    own = (groups * blocks + me * blocks + row).astype(jnp.float32)
    meta = jnp.where(lane == 0, own, jnp.where(lane <= nbr, listed, -1.0))
    meta = jnp.where(lane == 2 * tiles, spot.astype(jnp.float32), meta)
    meta = jnp.where(lane == 2 * tiles + 1, count.astype(jnp.float32), meta)
    rows = [held[n] for n in range(9)]
    mass = jnp.where(lane[:, 0:width] < count[:, 0:width], rows[6], 0.0)
    order = (rows[0], rows[1], rows[2], rows[7], mass, rows[3], rows[4], rows[5])
    for n in range(4):
        out[n * SUB : (n + 1) * SUB, :] = jnp.concatenate(order[2 * n : 2 * n + 2], axis=1)
    out[4 * SUB : 5 * SUB, :] = meta
    out[5 * SUB : 6 * SUB, :] = jnp.concatenate([rows[8], rows[6]], axis=1)


def place_region(groups, blocks, refs, rows, store):
    slab = groups * blocks
    me = lax.axis_index("seg")
    odd = lax.rem(lax.axis_index("dom"), 2)
    base_first = jnp.where(odd == 0, 2 * slab, 0)
    base_second = jnp.where(odd == 0, 0, 2 * slab)
    for k in range(groups):
        s = jnp.bitwise_xor(me, k)
        for base, ref, start in (
            (slab, refs[k], 0),
            (base_first, refs[groups], k * rows),
            (base_second, refs[groups + 1], k * rows),
        ):
            store(pl.multiple_of(base + s * blocks, SUB), ref, start)


def clear_tail(ref, first):
    if ref.shape[0] > first:
        ref[first:, :] = jnp.zeros((ref.shape[0] - first, ref.shape[1]), jnp.float32)


def parts_of(value):
    high = value.astype(jnp.bfloat16)
    rest = value - high.astype(jnp.float32)
    mid = rest.astype(jnp.bfloat16)
    return high, mid, (rest - mid.astype(jnp.float32)).astype(jnp.bfloat16)


def select(onehot, parts):
    total = None
    for part in reversed(parts):
        term = jnp.dot(onehot, part, preferred_element_type=jnp.float32)
        total = term if total is None else total + term
    return total


def far_fields(left, right, store):
    low = lane_iota(left.shape[0]) < HALF
    for n in range(left.shape[1] // LANES):
        one, two = left[:, n * LANES : (n + 1) * LANES], right[:, n * LANES : (n + 1) * LANES]
        store(2 * n, jnp.where(low, one, pltpu.roll(two, HALF, axis=1)))
        store(2 * n + 1, jnp.where(low, pltpu.roll(one, HALF, axis=1), two))


def column(value, index):
    at = index * SUB
    return jnp.broadcast_to(value[:, at : at + 1], (SUB, LANES))


def own_columns(cols, turned, d):
    turned[...] = pltpu.roll(cols[...], lax.rem(LANES - d, LANES), axis=1)


def group_rows(g):
    return slice(g * SUB, (g + 1) * SUB)


def put(result, g, slot, value):
    rows = group_rows(g)
    total = jnp.sum(value, axis=1, keepdims=True)
    result[rows, :] = jnp.where(lane_iota() == slot, total, result[rows, :])


def far_row(ref, field, tiles, d, t):
    return jnp.broadcast_to(ref[pl.ds((field * tiles + t) * SUB + d, 1), :], (SUB, LANES))


def each_slot(blocks, width, cols, turned, group):
    def slot(d, carry):
        own_columns(cols, turned, d)
        for g in range(width // SUB):
            group(d, g, turned[group_rows(g), :])
        return carry

    lax.fori_loop(0, blocks, slot, 0)


def sums_of(result, n, blocks, width):
    return jnp.transpose(result[...])[n * blocks : (n + 1) * blocks, 0:width]


def density_body(groups, blocks, width, tiles, *refs):
    parts = refs[: groups + 2]
    vol_out, rho_out, far, cols, own_rows, meta, hot, dist_out = refs[groups + 2 : groups + 10]
    region, own_range, own_tiles, turned, result = refs[groups + 10 :]
    slab = groups * blocks
    me = lax.axis_index("seg")
    kept = parts[groups].shape[0] // groups

    def store(at, ref, start):
        rows = pl.ds(at, SUB)
        for n in range(4):
            region[rows, n * LANES : (n + 1) * LANES] = ref[start + n * SUB : start + (n + 1) * SUB, :]
        meta[rows, :] = ref[start + 4 * SUB : start + 5 * SUB, :]

    place_region(groups, blocks, parts, kept, store)
    clear_tail(region, 3 * slab)
    clear_tail(meta, 3 * slab)
    for k in range(groups):
        rows = pl.ds(pl.multiple_of(jnp.bitwise_xor(me, k) * blocks, SUB), SUB)
        for n in range(6):
            own_range[rows, n * LANES : (n + 1) * LANES] = parts[k][n * SUB : (n + 1) * SUB, :]
    own_tiles[...] = jnp.zeros_like(own_tiles)
    result[...] = jnp.zeros_like(result)
    places = own_range[:, 4 * LANES + 2 * tiles : 4 * LANES + 2 * tiles + 1].astype(jnp.int32)
    wanted = me * blocks + lane_iota(slab)
    picks = jnp.where(jnp.broadcast_to(places, (slab, LANES)) == wanted, 1.0, 0.0)
    if slab < LANES:
        picks = jnp.concatenate([picks, jnp.zeros((LANES - slab, LANES), jnp.float32)], axis=0)
    picks = jnp.transpose(picks)[0:blocks, 0:slab].astype(jnp.bfloat16)
    mine = select(picks, parts_of(own_range[...]))
    entries = mine[:, 4 * LANES : 5 * LANES]
    for n in range(6):
        tile = mine[:, n * LANES : (n + 1) * LANES]
        if n == 4:
            continue
        at = 2 * n if n < 4 else 8
        own_rows[at] = tile
        own_rows[at + 1] = pltpu.roll(tile, HALF, axis=1)
    own_rows[10] = jnp.broadcast_to(entries[:, 2 * tiles + 1 : 2 * tiles + 2], (SUB, LANES))
    for n in range(8):
        own_tiles[n * SUB : (n + 1) * SUB, :] = own_rows[n]
    cols[...] = jnp.transpose(own_tiles[...])[0:width, :]
    size = region.shape[0]
    column_ids = lax.broadcasted_iota(jnp.int32, (SUB, size), 1)
    index = entries.astype(jnp.int32)
    for n in range(2 * tiles):
        chosen = jnp.broadcast_to(index[:, n : n + 1], (SUB, size)) == column_ids
        hot[n * SUB : (n + 1) * SUB, :] = jnp.where(chosen, 1.0, 0.0)
    values = parts_of(region[...])
    half = tiles * SUB
    left = select(hot[0:half, :].astype(jnp.bfloat16), values)
    right = select(hot[half:, :].astype(jnp.bfloat16), values)

    def keep(n, value):
        far[n * half : (n + 1) * half, :] = value

    far_fields(left, right, keep)

    def group(d, g, own):
        pos = [column(own, X + a) for a in range(3)]
        scale = 0.5 / column(own, SMOOTH)
        total = jnp.zeros((SUB, LANES), jnp.float32)
        for t in range(tiles):
            dx, dy, dz = [pos[a] - far_row(far, X + a, tiles, d, t) for a in range(3)]
            square = dx * dx + dy * dy + dz * dz
            dist = square * lax.rsqrt(jnp.maximum(square, TINY))
            dist_out[d, g, t] = dist
            ratio = dist * scale
            shell = jnp.maximum(1.0 - ratio, 0.0)
            shell = shell * shell
            shell = shell * shell
            total += shell * (far_row(far, MASS, tiles, d, t) * (0.25 + ratio))
        put(result, g, d, total)

    each_slot(blocks, width, cols, turned, group)
    sums = sums_of(result, 0, blocks, width)
    smooth, mass, count = [own_rows[n, :, 0:width] for n in (SMOOTH, MASS, 10)]
    live = jnp.where(lane_iota()[:, 0:width].astype(jnp.float32) < count, 1.0, 0.0)
    rho = 4.0 * SIGMA / (smooth * smooth * smooth) * sums + (1.0 - live)
    rho_out[...] = rho
    vol = mass / rho
    vol_out[...] = jnp.concatenate([vol, vol], axis=1)


def factor_body(groups, blocks, width, tiles, far, cols, meta, hot, dist, out, hot_out, turned):
    slab = groups * blocks
    size = hot.shape[1]
    spot = meta[:, 2 * tiles : 2 * tiles + 1].astype(jnp.int32)
    rows = lax.broadcasted_iota(jnp.int32, (size, size), 0)
    start = jnp.where(rows < slab, 0, jnp.where(rows < 2 * slab, slab, 2 * slab))
    chosen = start + spot == lax.broadcasted_iota(jnp.int32, (size, size), 1)
    moves = jnp.where(chosen, 1.0, 0.0).astype(jnp.bfloat16)
    hot_out[...] = jnp.dot(
        hot[...].astype(jnp.bfloat16), moves, preferred_element_type=jnp.float32
    )

    def group(d, g, own):
        smooth = column(own, SMOOTH)
        for t in range(tiles):
            inv = 1.0 / (smooth + far_row(far, SMOOTH, tiles, d, t))
            inv2 = inv * inv
            part = jnp.maximum(inv - dist[d, g, t] * inv2, 0.0)
            out[d, g, t] = part * part * part * inv2

    each_slot(blocks, width, cols, turned, group)


def tensor_body(groups, blocks, width, tiles, *refs):
    far, cols, own_rows, factor, hot, rho = refs[:6]
    vols = refs[6 : 8 + groups]
    coef_out, corr_out = refs[8 + groups : 10 + groups]
    turned, region, far_vol, result = refs[10 + groups :]
    slab = groups * blocks

    def store(at, ref, start):
        region[pl.ds(at, SUB), :] = ref[start : start + SUB, :]

    place_region(groups, blocks, vols, SUB, store)
    clear_tail(region, 3 * slab)
    result[...] = jnp.zeros_like(result)
    values = parts_of(region[...])
    half = tiles * SUB
    left = select(hot[0:half, :].astype(jnp.bfloat16), values)
    right = select(hot[half:, :].astype(jnp.bfloat16), values)
    far_vol[...] = jnp.where(lane_iota(half) < HALF, left, right)

    def group(d, g, own):
        pos = [column(own, X + a) for a in range(3)]
        total = [jnp.zeros((SUB, LANES), jnp.float32) for _ in range(6)]
        for t in range(tiles):
            dx, dy, dz = [pos[a] - far_row(far, X + a, tiles, d, t) for a in range(3)]
            weight = factor[d, g, t] * far_row(far_vol, 0, tiles, d, t)
            wx, wy, wz = weight * dx, weight * dy, weight * dz
            for n, term in enumerate((wx * dx, wy * dy, wz * dz, wx * dy, wx * dz, wy * dz)):
                total[n] += term
        for n in range(6):
            put(result, g, n * blocks + d, total[n])

    each_slot(blocks, width, cols, turned, group)
    sums = jnp.transpose(result[...])
    press = GAMMA_LESS * own_rows[8, :, 0:width] / rho[...]
    scale = own_rows[MASS, :, 0:width] * press
    coefs = []
    for n in range(6):
        tensor = SLOPE * sums[n * blocks : (n + 1) * blocks, 0:width]
        corr = (2.0 + tensor) if n < 3 else tensor
        corr_out[n] = corr
        coefs.append(scale * corr)
    corr_out[6] = press
    for n in range(3):
        coef_out[n * SUB : (n + 1) * SUB, :] = jnp.concatenate(coefs[2 * n : 2 * n + 2], axis=1)


def moment_body(blocks, width, tiles, far, cols, factor, out, slopes, turned, result):
    result[...] = jnp.zeros_like(result)

    def group(d, g, own):
        pos = [column(own, X + a) for a in range(3)]
        vel = [column(own, VEL + a) for a in range(3)]
        total = [jnp.zeros((SUB, LANES), jnp.float32) for _ in range(9)]
        for t in range(tiles):
            weight = factor[d, g, t]
            mass = far_row(far, MASS, tiles, d, t)
            slope = [weight * (pos[a] - far_row(far, X + a, tiles, d, t)) for a in range(3)]
            for a in range(3):
                slopes[a, d, g, t] = slope[a]
            px, py, pz = [mass * slope[a] for a in range(3)]
            vx, vy, vz = [vel[a] - far_row(far, VEL + a, tiles, d, t) for a in range(3)]
            terms = (
                px,
                py,
                pz,
                vx * px,
                vy * py,
                vz * pz,
                vx * py + vy * px,
                vx * pz + vz * px,
                vy * pz + vz * py,
            )
            for n, term in enumerate(terms):
                total[n] += term
        for n in range(9):
            put(result, g, n * blocks + d, total[n])

    each_slot(blocks, width, cols, turned, group)
    sums = jnp.transpose(result[...])
    for n in range(9):
        out[n] = sums[n * blocks : (n + 1) * blocks, 0:width]


def update_body(groups, blocks, width, tiles, *refs):
    own_rows, slopes, hot, corr, moments = refs[:5]
    coefs = refs[5 : 7 + groups]
    state_out = refs[7 + groups]
    region, far_coef, result = refs[8 + groups :]
    slab = groups * blocks

    def store(at, ref, start):
        for n in range(3):
            tile = ref[start + n * SUB : start + (n + 1) * SUB, :]
            region[pl.ds(at, SUB), n * LANES : (n + 1) * LANES] = tile

    place_region(groups, blocks, coefs, 3 * SUB, store)
    clear_tail(region, 3 * slab)
    result[...] = jnp.zeros_like(result)
    values = parts_of(region[...])
    half = tiles * SUB
    left = select(hot[0:half, :].astype(jnp.bfloat16), values)
    right = select(hot[half:, :].astype(jnp.bfloat16), values)

    def keep(n, value):
        far_coef[n * half : (n + 1) * half, :] = value

    far_fields(left, right, keep)

    def slot(d, carry):
        for g in range(width // SUB):
            total = [jnp.zeros((SUB, LANES), jnp.float32) for _ in range(3)]
            for t in range(tiles):
                ex, ey, ez = [slopes[a, d, g, t] for a in range(3)]
                xx, yy, zz, xy, xz, yz = [far_row(far_coef, n, tiles, d, t) for n in range(6)]
                total[0] += xx * ex + xy * ey + xz * ez
                total[1] += xy * ex + yy * ey + yz * ez
                total[2] += xz * ex + yz * ey + zz * ez
            for n in range(3):
                put(result, g, n * blocks + d, total[n])
        return carry

    lax.fori_loop(0, blocks, slot, 0)
    sums = jnp.transpose(result[...])
    field = lambda n: own_rows[n, :, 0:width]
    live = jnp.where(lane_iota()[:, 0:width].astype(jnp.float32) < field(10), 1.0, 0.0)
    press = corr[6]
    xx, yy, zz, xy, xz, yz = [corr[n] for n in range(6)]
    sx, sy, sz = [moments[n] for n in range(3)]
    near = (xx * sx + xy * sy + xz * sz, xy * sx + yy * sy + yz * sz, xz * sx + yz * sy + zz * sz)
    for a in range(3):
        far_sum = sums[a * blocks : (a + 1) * blocks, 0:width]
        accel = -SLOPE * live * (press * near[a] + far_sum)
        velocity = field(VEL + a) + STEP_DT * accel
        state_out[3 + a] = velocity
        state_out[a] = field(X + a) + STEP_DT * velocity
    heat = moments[3] * xx + moments[4] * yy + moments[5] * zz
    heat += moments[6] * xy + moments[7] * xz + moments[8] * yz
    state_out[6] = field(9)
    state_out[7] = field(SMOOTH)
    state_out[8] = field(8) + STEP_DT * (SLOPE * live * press * heat)


def exchange(own, send_rows):
    groups = lax.axis_size("seg")
    ranges = lax.axis_size("dom")
    seg = [own]
    for k in range(1, groups):
        seg.append(lax.ppermute(own, "seg", [(i, i ^ k) for i in range(groups)]))
    whole = jnp.concatenate([part[:send_rows] for part in seg], axis=0)
    first = [(i, i ^ 1) for i in range(ranges)]
    second = [(i, ((i + 1) ^ 1) - 1) for i in range(1, ranges - 1)]
    return seg + [lax.ppermute(whole, "dom", first), lax.ppermute(whole, "dom", second)]


def local(state, counts, neighbours, new_place):
    blocks, fields, width = state.shape
    nbr = neighbours.shape[1]
    groups = lax.axis_size("seg")
    slab = blocks * groups
    tiles = (nbr + 2) // 2
    size = -(-3 * slab // LANES) * LANES
    many = (blocks, width // SUB, tiles, SUB, LANES)
    f32, i32 = jnp.float32, jnp.int32
    vm = pl.BlockSpec(memory_space=VMEM)
    any_space = pl.BlockSpec(memory_space=pltpu.HBM)
    columns = VMEM((width, LANES), f32)
    packed = call(
        functools.partial(pack_body, blocks, width, nbr, tiles),
        shape(6 * SUB, LANES),
        in_specs=[any_space] * 4,
        out_specs=vm,
        scratch=(
            VMEM((fields, blocks, width), f32),
            VMEM((blocks, nbr), i32),
            SMEM((blocks,), i32),
            SMEM((blocks,), i32),
            pltpu.SemaphoreType.DMA((4,)),
        ),
        name="pack",
    )(counts, new_place, jnp.swapaxes(state, 0, 1), neighbours)
    parts = exchange(packed, 5 * SUB)
    vol, rho, far, cols, own_rows, meta, hot, dist = call(
        functools.partial(density_body, groups, blocks, width, tiles),
        (
            shape(SUB, LANES),
            shape(blocks, width),
            shape(8 * tiles * SUB, LANES),
            shape(width, LANES),
            shape(11, SUB, LANES),
            shape(size, LANES),
            shape(2 * tiles * SUB, size),
            shape(*many),
        ),
        in_specs=[vm] * (groups + 2),
        out_specs=(vm,) * 8,
        scratch=(
            VMEM((size, 4 * LANES), f32),
            VMEM((slab, 6 * LANES), f32),
            VMEM((LANES, LANES), f32),
            columns,
            columns,
        ),
        name="density",
    )(*parts)
    vols = exchange(vol, SUB)
    factor, placed = call(
        functools.partial(factor_body, groups, blocks, width, tiles),
        (shape(*many), shape(2 * tiles * SUB, size)),
        in_specs=[vm] * 5,
        out_specs=(vm, vm),
        scratch=(columns,),
        name="factor",
    )(far, cols, meta, hot, dist)
    coef, corr = call(
        functools.partial(tensor_body, groups, blocks, width, tiles),
        (shape(3 * SUB, LANES), shape(7, blocks, width)),
        in_specs=[vm] * (6 + groups + 2),
        out_specs=(vm, vm),
        scratch=(columns, VMEM((size, LANES), f32), VMEM((tiles * SUB, LANES), f32), columns),
        name="tensor",
    )(far, cols, own_rows, factor, placed, rho, *vols)
    coefs = exchange(coef, 3 * SUB)
    moments, slopes = call(
        functools.partial(moment_body, blocks, width, tiles),
        (shape(9, blocks, width), shape(3, *many)),
        in_specs=[vm] * 3,
        out_specs=(vm, vm),
        scratch=(columns, columns),
        name="moments",
    )(far, cols, factor)
    moved = call(
        functools.partial(update_body, groups, blocks, width, tiles),
        shape(fields, blocks, width),
        in_specs=[vm] * (5 + groups + 2),
        out_specs=vm,
        scratch=(
            VMEM((size, 3 * LANES), f32),
            VMEM((6 * tiles * SUB, LANES), f32),
            columns,
        ),
        name="update",
    )(own_rows, slopes, placed, corr, moments, *coefs)
    return (jnp.swapaxes(moved, 0, 1), rho)


def solution(mesh):
    return jax.shard_map(
        local,
        mesh=mesh,
        in_specs=(
            P(("dom", "seg"), None, None),
            P(("dom", "seg")),
            P(("dom", "seg"), None),
            P(("dom", "seg")),
        ),
        out_specs=(P(("dom", "seg"), None, None), P(("dom", "seg"), None)),
        check_vma=False,
    )
```

```python
import functools
import math

import jax
import jax.numpy as jnp
from jax import lax
from jax.experimental import pallas as pl
from jax.experimental.pallas import tpu as pltpu
from jax.sharding import PartitionSpec as P


SIGMA = 21.0 / (16.0 * math.pi)
GAMMA_LESS = 2.0 / 3.0
STEP_DT = 0.1
SLOPE = -5.0 * SIGMA * 32.0
TINY = 1e-37
SPLIT = (2, 6, 8)
SUB = 8
LANES = 128
X, SMOOTH, MASS, VEL = 0, 3, 4, 5
HALF = LANES // 2
VMEM = pltpu.VMEM
SMEM = pltpu.SMEM


def lane_iota(rows=SUB):
    return lax.broadcasted_iota(jnp.int32, (rows, LANES), 1)


def row_iota(rows=SUB):
    return lax.broadcasted_iota(jnp.int32, (rows, LANES), 0)


def call(body, outs, scratch=(), in_specs=None, out_specs=None, grant=8):
    return pl.pallas_call(
        body,
        out_shape=outs,
        in_specs=in_specs,
        out_specs=out_specs,
        scratch_shapes=list(scratch),
        compiler_params=pltpu.CompilerParams(vmem_limit_bytes=grant << 20),
    )


def shape(*dims, dtype=jnp.float32):
    return jax.ShapeDtypeStruct(dims, dtype)


def pack_body(blocks, width, nbr, tiles, *refs):
    counts, place, state, lists, out, held, entries, few, ids, sem = refs
    copies = [
        pltpu.make_async_copy(source, target, sem.at[n])
        for n, (source, target) in enumerate(
            ((state, held), (lists, entries), (counts, few), (place, ids))
        )
    ]
    for copy in copies:
        copy.start()
    for copy in copies:
        copy.wait()
    groups = lax.axis_size("seg")
    me = lax.axis_index("seg")
    lane, row = lane_iota(), row_iota()
    count = jnp.zeros((SUB, LANES), jnp.int32)
    spot = jnp.zeros((SUB, LANES), jnp.int32)
    for b in range(blocks):
        count = jnp.where(row == b, few[b], count)
        spot = jnp.where(row == b, ids[b], spot)
    listed = jnp.concatenate(
        [entries[...], jnp.zeros((blocks, LANES - nbr), jnp.int32)], axis=1
    ).astype(jnp.float32)
    listed = pltpu.roll(listed, 1, axis=1)
    own = (groups * blocks + me * blocks + row).astype(jnp.float32)
    meta = jnp.where(lane == 0, own, jnp.where(lane <= nbr, listed, -1.0))
    meta = jnp.where(lane == 2 * tiles, spot.astype(jnp.float32), meta)
    meta = jnp.where(lane == 2 * tiles + 1, count.astype(jnp.float32), meta)
    rows = [held[n] for n in range(9)]
    mass = jnp.where(lane[:, 0:width] < count[:, 0:width], rows[6], 0.0)
    order = (rows[0], rows[1], rows[2], rows[7], mass, rows[3], rows[4], rows[5])
    for n in range(4):
        out[n * SUB : (n + 1) * SUB, :] = jnp.concatenate(order[2 * n : 2 * n + 2], axis=1)
    out[4 * SUB : 5 * SUB, :] = meta
    out[5 * SUB : 6 * SUB, :] = jnp.concatenate([rows[8], rows[6]], axis=1)


def place_region(groups, blocks, refs, rows, region, store):
    slab = groups * blocks
    me = lax.axis_index("seg")
    odd = lax.rem(lax.axis_index("dom"), 2)
    base_first = jnp.where(odd == 0, 2 * slab, 0)
    base_second = jnp.where(odd == 0, 0, 2 * slab)
    for k in range(groups):
        s = jnp.bitwise_xor(me, k)
        for base, ref, start in (
            (slab, refs[k], 0),
            (base_first, refs[groups], k * rows),
            (base_second, refs[groups + 1], k * rows),
        ):
            store(pl.multiple_of(base + s * blocks, SUB), ref, start)
    at_end = (lax.axis_index("dom") == 0) | (lax.axis_index("dom") == lax.axis_size("dom") - 1)

    @pl.when(at_end)
    def _():
        rows = pl.ds(pl.multiple_of(base_second, SUB), slab)
        region[rows, :] = jnp.zeros((slab, region.shape[1]), jnp.float32)

    clear_tail(region, 3 * slab)


def clear_tail(ref, first):
    if ref.shape[0] > first:
        ref[first:, :] = jnp.zeros((ref.shape[0] - first, ref.shape[1]), jnp.float32)


def parts_of(value):
    high = value.astype(jnp.bfloat16)
    rest = value - high.astype(jnp.float32)
    mid = rest.astype(jnp.bfloat16)
    return high, mid, (rest - mid.astype(jnp.float32)).astype(jnp.bfloat16)


def select(onehot, parts):
    total = None
    for part in reversed(parts):
        term = jnp.dot(onehot, part, preferred_element_type=jnp.float32)
        total = term if total is None else total + term
    return total


def far_fields(left, right, store):
    low = lane_iota(left.shape[0]) < HALF
    for n in range(left.shape[1] // LANES):
        one, two = left[:, n * LANES : (n + 1) * LANES], right[:, n * LANES : (n + 1) * LANES]
        store(2 * n, jnp.where(low, one, pltpu.roll(two, HALF, axis=1)))
        store(2 * n + 1, jnp.where(low, pltpu.roll(one, HALF, axis=1), two))


def column(value, index):
    at = index * SUB
    return jnp.broadcast_to(value[:, at : at + 1], (SUB, LANES))


def own_columns(cols, turned, d):
    turned[...] = pltpu.roll(cols[...], lax.rem(LANES - d, LANES), axis=1)


def group_rows(g):
    return slice(g * SUB, (g + 1) * SUB)


def put(result, g, slot, value):
    rows = group_rows(g)
    total = jnp.sum(value, axis=1, keepdims=True)
    result[rows, :] = jnp.where(lane_iota() == slot, total, result[rows, :])


def far_row(ref, field, tiles, d, t):
    return jnp.broadcast_to(ref[pl.ds((field * tiles + t) * SUB + d, 1), :], (SUB, LANES))


def each_slot(first, count, width, cols, turned, group):
    def slot(d, carry):
        own_columns(cols, turned, first + d)
        for g in range(width // SUB):
            group(d, g, turned[group_rows(g), :])
        return carry

    lax.fori_loop(0, count, slot, 0)


def sums_of(result, n, blocks, width):
    return jnp.transpose(result[...])[n * blocks : (n + 1) * blocks, 0:width]


def density_body(groups, blocks, width, tiles, *refs):
    parts = refs[: groups + 2]
    vol_out, rho_out, far, cols, own_rows, meta, hot, dist_out = refs[groups + 2 : groups + 10]
    region, own_range, own_tiles, turned, result = refs[groups + 10 :]
    slab = groups * blocks
    me = lax.axis_index("seg")
    kept = parts[groups].shape[0] // groups

    def store(at, ref, start):
        rows = pl.ds(at, SUB)
        for n in range(4):
            region[rows, n * LANES : (n + 1) * LANES] = ref[start + n * SUB : start + (n + 1) * SUB, :]
        meta[rows, :] = ref[start + 4 * SUB : start + 5 * SUB, :]

    place_region(groups, blocks, parts, kept, region, store)
    clear_tail(meta, 3 * slab)
    for k in range(groups):
        rows = pl.ds(pl.multiple_of(jnp.bitwise_xor(me, k) * blocks, SUB), SUB)
        for n in range(6):
            own_range[rows, n * LANES : (n + 1) * LANES] = parts[k][n * SUB : (n + 1) * SUB, :]
    own_tiles[...] = jnp.zeros_like(own_tiles)
    result[...] = jnp.zeros_like(result)
    places = own_range[:, 4 * LANES + 2 * tiles : 4 * LANES + 2 * tiles + 1].astype(jnp.int32)
    wanted = me * blocks + lane_iota(slab)
    picks = jnp.where(jnp.broadcast_to(places, (slab, LANES)) == wanted, 1.0, 0.0)
    if slab < LANES:
        picks = jnp.concatenate([picks, jnp.zeros((LANES - slab, LANES), jnp.float32)], axis=0)
    picks = jnp.transpose(picks)[0:blocks, 0:slab].astype(jnp.bfloat16)
    mine = select(picks, parts_of(own_range[...]))
    entries = mine[:, 4 * LANES : 5 * LANES]
    for n in range(6):
        tile = mine[:, n * LANES : (n + 1) * LANES]
        if n == 4:
            continue
        at = 2 * n if n < 4 else 8
        own_rows[at] = tile
        own_rows[at + 1] = pltpu.roll(tile, HALF, axis=1)
    own_rows[10] = jnp.broadcast_to(entries[:, 2 * tiles + 1 : 2 * tiles + 2], (SUB, LANES))
    for n in range(8):
        own_tiles[n * SUB : (n + 1) * SUB, :] = own_rows[n]
    cols[...] = jnp.transpose(own_tiles[...])[0:width, :]
    size = region.shape[0]
    column_ids = lax.broadcasted_iota(jnp.int32, (SUB, size), 1)
    index = entries.astype(jnp.int32)
    for n in range(2 * tiles):
        chosen = jnp.broadcast_to(index[:, n : n + 1], (SUB, size)) == column_ids
        hot[n * SUB : (n + 1) * SUB, :] = jnp.where(chosen, 1.0, 0.0)
    values = parts_of(region[...])
    half = tiles * SUB
    left = select(hot[0:half, :].astype(jnp.bfloat16), values)
    right = select(hot[half:, :].astype(jnp.bfloat16), values)

    def keep(n, value):
        far[n * half : (n + 1) * half, :] = value

    far_fields(left, right, keep)

    def group(d, g, own):
        pos = [column(own, X + a) for a in range(3)]
        scale = 0.5 / column(own, SMOOTH)
        total = jnp.zeros((SUB, LANES), jnp.float32)
        for t in range(tiles):
            dx, dy, dz = [pos[a] - far_row(far, X + a, tiles, d, t) for a in range(3)]
            square = dx * dx + dy * dy + dz * dz
            dist = square * lax.rsqrt(jnp.maximum(square, TINY))
            dist_out[d, g, t] = dist
            ratio = dist * scale
            shell = jnp.maximum(1.0 - ratio, 0.0)
            shell = shell * shell
            shell = shell * shell
            total += shell * (far_row(far, MASS, tiles, d, t) * (0.25 + ratio))
        put(result, g, d, total)

    each_slot(0, blocks, width, cols, turned, group)
    sums = sums_of(result, 0, blocks, width)
    smooth, mass, count = [own_rows[n, :, 0:width] for n in (SMOOTH, MASS, 10)]
    live = jnp.where(lane_iota()[:, 0:width].astype(jnp.float32) < count, 1.0, 0.0)
    rho = 4.0 * SIGMA / (smooth * smooth * smooth) * sums + (1.0 - live)
    rho_out[...] = rho
    vol = mass / rho
    vol_out[...] = jnp.concatenate([vol, vol], axis=1)


def factor_body(groups, blocks, width, tiles, far, cols, meta, hot, dist, out, hot_out, turned):
    slab = groups * blocks
    size = hot.shape[1]
    spot = meta[:, 2 * tiles : 2 * tiles + 1].astype(jnp.int32)
    rows = lax.broadcasted_iota(jnp.int32, (size, size), 0)
    start = jnp.where(rows < slab, 0, jnp.where(rows < 2 * slab, slab, 2 * slab))
    chosen = start + spot == lax.broadcasted_iota(jnp.int32, (size, size), 1)
    moves = jnp.where(chosen, 1.0, 0.0).astype(jnp.bfloat16)
    hot_out[...] = jnp.dot(
        hot[...].astype(jnp.bfloat16), moves, preferred_element_type=jnp.float32
    )

    def group(d, g, own):
        smooth = column(own, SMOOTH)
        for t in range(tiles):
            inv = 1.0 / (smooth + far_row(far, SMOOTH, tiles, d, t))
            inv2 = inv * inv
            part = jnp.maximum(inv - dist[d, g, t] * inv2, 0.0)
            out[d, g, t] = part * part * part * inv2

    each_slot(0, blocks, width, cols, turned, group)


def tensor_body(groups, blocks, width, tiles, *refs):
    far, cols, own_rows, factor, hot, rho = refs[:6]
    vols = refs[6 : 8 + groups]
    coef_out, corr_out = refs[8 + groups : 10 + groups]
    turned, region, far_vol, result = refs[10 + groups :]

    def store(at, ref, start):
        region[pl.ds(at, SUB), :] = ref[start : start + SUB, :]

    place_region(groups, blocks, vols, SUB, region, store)
    result[...] = jnp.zeros_like(result)
    values = parts_of(region[...])
    half = tiles * SUB
    left = select(hot[0:half, :].astype(jnp.bfloat16), values)
    right = select(hot[half:, :].astype(jnp.bfloat16), values)
    far_vol[...] = jnp.where(lane_iota(half) < HALF, left, right)

    def group(d, g, own):
        pos = [column(own, X + a) for a in range(3)]
        total = [jnp.zeros((SUB, LANES), jnp.float32) for _ in range(6)]
        for t in range(tiles):
            dx, dy, dz = [pos[a] - far_row(far, X + a, tiles, d, t) for a in range(3)]
            weight = factor[d, g, t] * far_row(far_vol, 0, tiles, d, t)
            wx, wy, wz = weight * dx, weight * dy, weight * dz
            for n, term in enumerate((wx * dx, wy * dy, wz * dz, wx * dy, wx * dz, wy * dz)):
                total[n] += term
        for n in range(6):
            put(result, g, n * blocks + d, total[n])

    each_slot(0, blocks, width, cols, turned, group)
    sums = jnp.transpose(result[...])
    press = GAMMA_LESS * own_rows[8, :, 0:width] / rho[...]
    scale = own_rows[MASS, :, 0:width] * press
    coefs = []
    for n in range(6):
        tensor = SLOPE * sums[n * blocks : (n + 1) * blocks, 0:width]
        corr = (2.0 + tensor) if n < 3 else tensor
        corr_out[n] = corr
        coefs.append(scale * corr)
    corr_out[6] = press
    for n in range(3):
        coef_out[n * SUB : (n + 1) * SUB, :] = jnp.concatenate(coefs[2 * n : 2 * n + 2], axis=1)


def moment_body(first, count, blocks, width, tiles, far, cols, factor, out, slopes, turned, result):
    result[...] = jnp.zeros_like(result)

    def group(d, g, own):
        at = first + d
        pos = [column(own, X + a) for a in range(3)]
        vel = [column(own, VEL + a) for a in range(3)]
        total = [jnp.zeros((SUB, LANES), jnp.float32) for _ in range(9)]
        for t in range(tiles):
            weight = factor[at, g, t]
            mass = far_row(far, MASS, tiles, at, t)
            slope = [weight * (pos[a] - far_row(far, X + a, tiles, at, t)) for a in range(3)]
            for a in range(3):
                slopes[a, d, g, t] = slope[a]
            px, py, pz = [mass * slope[a] for a in range(3)]
            vx, vy, vz = [vel[a] - far_row(far, VEL + a, tiles, at, t) for a in range(3)]
            terms = (
                px,
                py,
                pz,
                vx * px,
                vy * py,
                vz * pz,
                vx * py + vy * px,
                vx * pz + vz * px,
                vy * pz + vz * py,
            )
            for n, term in enumerate(terms):
                total[n] += term
        for n in range(9):
            put(result, g, n * blocks + at, total[n])

    each_slot(first, count, width, cols, turned, group)
    sums = jnp.transpose(result[...])
    for n in range(9):
        out[n] = sums[n * blocks : (n + 1) * blocks, 0:width]


def update_body(spans, groups, blocks, width, tiles, *refs):
    own_rows, hot, corr = refs[:3]
    pieces, refs = refs[3 : 3 + 2 * len(spans)], refs[3 + 2 * len(spans) :]
    coefs = refs[: 2 + groups]
    state_out = refs[2 + groups]
    region, far_coef, result = refs[3 + groups :]

    def store(at, ref, start):
        for n in range(3):
            tile = ref[start + n * SUB : start + (n + 1) * SUB, :]
            region[pl.ds(at, SUB), n * LANES : (n + 1) * LANES] = tile

    place_region(groups, blocks, coefs, 3 * SUB, region, store)
    result[...] = jnp.zeros_like(result)
    values = parts_of(region[...])
    half = tiles * SUB
    left = select(hot[0:half, :].astype(jnp.bfloat16), values)
    right = select(hot[half:, :].astype(jnp.bfloat16), values)

    def keep(n, value):
        far_coef[n * half : (n + 1) * half, :] = value

    far_fields(left, right, keep)

    def slot(first, slopes, d, carry):
        at = first + d
        for g in range(width // SUB):
            total = [jnp.zeros((SUB, LANES), jnp.float32) for _ in range(3)]
            for t in range(tiles):
                ex, ey, ez = [slopes[a, d, g, t] for a in range(3)]
                xx, yy, zz, xy, xz, yz = [far_row(far_coef, n, tiles, at, t) for n in range(6)]
                total[0] += xx * ex + xy * ey + xz * ez
                total[1] += xy * ex + yy * ey + yz * ez
                total[2] += xz * ex + yz * ey + zz * ez
            for n in range(3):
                put(result, g, n * blocks + at, total[n])
        return carry

    for n, (first, count) in enumerate(spans):
        lax.fori_loop(0, count, functools.partial(slot, first, pieces[2 * n + 1]), 0)
    moments = [sum(pieces[2 * n][m] for n in range(len(spans))) for m in range(9)]
    sums = jnp.transpose(result[...])
    field = lambda n: own_rows[n, :, 0:width]
    live = jnp.where(lane_iota()[:, 0:width].astype(jnp.float32) < field(10), 1.0, 0.0)
    press = corr[6]
    xx, yy, zz, xy, xz, yz = [corr[n] for n in range(6)]
    sx, sy, sz = [moments[n] for n in range(3)]
    near = (xx * sx + xy * sy + xz * sz, xy * sx + yy * sy + yz * sz, xz * sx + yz * sy + zz * sz)
    for a in range(3):
        far_sum = sums[a * blocks : (a + 1) * blocks, 0:width]
        accel = -SLOPE * live * (press * near[a] + far_sum)
        velocity = field(VEL + a) + STEP_DT * accel
        state_out[3 + a] = velocity
        state_out[a] = field(X + a) + STEP_DT * velocity
    heat = moments[3] * xx + moments[4] * yy + moments[5] * zz
    heat += moments[6] * xy + moments[7] * xz + moments[8] * yz
    state_out[6] = field(9)
    state_out[7] = field(SMOOTH)
    state_out[8] = field(8) + STEP_DT * (SLOPE * live * press * heat)


def exchange(own, send_rows):
    groups = lax.axis_size("seg")
    ranges = lax.axis_size("dom")
    seg = [own]
    for k in range(1, groups):
        seg.append(lax.ppermute(own, "seg", [(i, i ^ k) for i in range(groups)]))
    whole = jnp.concatenate([part[:send_rows] for part in seg], axis=0)
    first = [(i, i ^ 1) for i in range(ranges)]
    second = []
    for r in range(ranges):
        for s in range(groups):
            inside = 0 < r < ranges - 1
            other = (((r + 1) ^ 1) - 1) * groups + s if inside else r * groups + (s ^ 1)
            second.append((r * groups + s, other))
    return seg + [lax.ppermute(whole, "dom", first), lax.ppermute(whole, ("dom", "seg"), second)]


def step(state, counts, neighbours, new_place):
    blocks, fields, width = state.shape
    nbr = neighbours.shape[1]
    groups = lax.axis_size("seg")
    slab = blocks * groups
    tiles = (nbr + 2) // 2
    size = -(-3 * slab // LANES) * LANES
    many = (blocks, width // SUB, tiles, SUB, LANES)
    f32, i32 = jnp.float32, jnp.int32
    vm = pl.BlockSpec(memory_space=VMEM)
    any_space = pl.BlockSpec(memory_space=pltpu.HBM)
    columns = VMEM((width, LANES), f32)
    packed = call(
        functools.partial(pack_body, blocks, width, nbr, tiles),
        shape(6 * SUB, LANES),
        in_specs=[any_space] * 4,
        out_specs=vm,
        scratch=(
            VMEM((fields, blocks, width), f32),
            VMEM((blocks, nbr), i32),
            SMEM((blocks,), i32),
            SMEM((blocks,), i32),
            pltpu.SemaphoreType.DMA((4,)),
        ),
    )(*[
        pltpu.with_memory_space_constraint(value, pltpu.HBM)
        for value in (counts, new_place, jnp.swapaxes(state, 0, 1), neighbours)
    ])
    parts = exchange(packed, 5 * SUB)
    vol, rho, far, cols, own_rows, meta, hot, dist = call(
        functools.partial(density_body, groups, blocks, width, tiles),
        (
            shape(SUB, LANES),
            shape(blocks, width),
            shape(8 * tiles * SUB, LANES),
            shape(width, LANES),
            shape(11, SUB, LANES),
            shape(size, LANES),
            shape(2 * tiles * SUB, size),
            shape(*many),
        ),
        in_specs=[vm] * (groups + 2),
        out_specs=(vm,) * 8,
        scratch=(
            VMEM((size, 4 * LANES), f32),
            VMEM((slab, 6 * LANES), f32),
            VMEM((LANES, LANES), f32),
            columns,
            columns,
        ),
    )(*parts)
    vols = exchange(vol, SUB)
    factor, placed = call(
        functools.partial(factor_body, groups, blocks, width, tiles),
        (shape(*many), shape(2 * tiles * SUB, size)),
        in_specs=[vm] * 5,
        out_specs=(vm, vm),
        scratch=(columns,),
    )(far, cols, meta, hot, dist)
    coef, corr = call(
        functools.partial(tensor_body, groups, blocks, width, tiles),
        (shape(3 * SUB, LANES), shape(7, blocks, width)),
        in_specs=[vm] * (6 + groups + 2),
        out_specs=(vm, vm),
        scratch=(columns, VMEM((size, LANES), f32), VMEM((tiles * SUB, LANES), f32), columns),
    )(far, cols, own_rows, factor, placed, rho, *vols)
    coefs = exchange(coef, 3 * SUB)
    ends = [blocks * n // SUB for n in (0,) + SPLIT]
    spans = [(low, high - low) for low, high in zip(ends, ends[1:])]
    pieces = []
    for first_slot, count in spans:
        pieces += call(
            functools.partial(moment_body, first_slot, count, blocks, width, tiles),
            (shape(9, blocks, width), shape(3, count, *many[1:])),
            in_specs=[vm] * 3,
            out_specs=(vm, vm),
            scratch=(columns, columns),
        )(far, cols, factor)
    moved = call(
        functools.partial(update_body, spans, groups, blocks, width, tiles),
        shape(fields, blocks, width),
        in_specs=[vm] * (3 + len(pieces) + groups + 2),
        out_specs=vm,
        scratch=(
            VMEM((size, 3 * LANES), f32),
            VMEM((6 * tiles * SUB, LANES), f32),
            columns,
        ),
    )(own_rows, placed, corr, *pieces, *coefs)
    return (jnp.swapaxes(moved, 0, 1), rho)


def solution(mesh):
    return jax.shard_map(
        step,
        mesh=mesh,
        in_specs=(
            P(("dom", "seg"), None, None),
            P(("dom", "seg")),
            P(("dom", "seg"), None),
            P(("dom", "seg")),
        ),
        out_specs=(P(("dom", "seg"), None, None), P(("dom", "seg"), None)),
        check_vma=False,
    )
```

```python
import functools
import math

import jax
import jax.numpy as jnp
from jax import lax
from jax.experimental import pallas as pl
from jax.experimental.pallas import tpu as pltpu
from jax.sharding import PartitionSpec as P


SIGMA = 21.0 / (16.0 * math.pi)
GAMMA_LESS = 2.0 / 3.0
STEP_DT = 0.1
SLOPE = -5.0 * SIGMA * 32.0
TINY = 1e-37
FACTOR_SPLIT = (5, 8)
MOMENT_SPLIT = (5, 8)
SUB = 8
LANES = 128
X, SMOOTH, MASS, VEL = 0, 3, 4, 5
HALF = LANES // 2
VMEM = pltpu.VMEM
SMEM = pltpu.SMEM


def lane_iota(rows=SUB):
    return lax.broadcasted_iota(jnp.int32, (rows, LANES), 1)


def row_iota(rows=SUB):
    return lax.broadcasted_iota(jnp.int32, (rows, LANES), 0)


def call(body, outs, scratch=(), in_specs=None, out_specs=None, grant=8):
    return pl.pallas_call(
        body,
        out_shape=outs,
        in_specs=in_specs,
        out_specs=out_specs,
        scratch_shapes=list(scratch),
        compiler_params=pltpu.CompilerParams(vmem_limit_bytes=grant << 20),
    )


def shape(*dims, dtype=jnp.float32):
    return jax.ShapeDtypeStruct(dims, dtype)


def pack_body(blocks, width, nbr, tiles, *refs):
    counts, place, state, lists, out, held, entries, few, ids, sem = refs
    copies = [
        pltpu.make_async_copy(source, target, sem.at[n])
        for n, (source, target) in enumerate(
            ((state, held), (lists, entries), (counts, few), (place, ids))
        )
    ]
    for copy in copies:
        copy.start()
    for copy in copies:
        copy.wait()
    groups = lax.axis_size("seg")
    me = lax.axis_index("seg")
    lane, row = lane_iota(), row_iota()
    count = jnp.zeros((SUB, LANES), jnp.int32)
    spot = jnp.zeros((SUB, LANES), jnp.int32)
    for b in range(blocks):
        count = jnp.where(row == b, few[b], count)
        spot = jnp.where(row == b, ids[b], spot)
    listed = jnp.concatenate(
        [entries[...], jnp.zeros((blocks, LANES - nbr), jnp.int32)], axis=1
    ).astype(jnp.float32)
    listed = pltpu.roll(listed, 1, axis=1)
    own = (groups * blocks + me * blocks + row).astype(jnp.float32)
    meta = jnp.where(lane == 0, own, jnp.where(lane <= nbr, listed, -1.0))
    meta = jnp.where(lane == 2 * tiles, spot.astype(jnp.float32), meta)
    meta = jnp.where(lane == 2 * tiles + 1, count.astype(jnp.float32), meta)
    rows = [held[n] for n in range(9)]
    mass = jnp.where(lane[:, 0:width] < count[:, 0:width], rows[6], 0.0)
    order = (rows[0], rows[1], rows[2], rows[7], mass, rows[3], rows[4], rows[5])
    for n in range(4):
        out[n * SUB : (n + 1) * SUB, :] = jnp.concatenate(order[2 * n : 2 * n + 2], axis=1)
    out[4 * SUB : 5 * SUB, :] = meta
    out[5 * SUB : 6 * SUB, :] = jnp.concatenate([rows[8], rows[6]], axis=1)


def place_region(groups, blocks, refs, rows, region, store):
    slab = groups * blocks
    me = lax.axis_index("seg")
    odd = lax.rem(lax.axis_index("dom"), 2)
    base_first = jnp.where(odd == 0, 2 * slab, 0)
    base_second = jnp.where(odd == 0, 0, 2 * slab)
    for k in range(groups):
        s = jnp.bitwise_xor(me, k)
        for base, ref, start in (
            (slab, refs[k], 0),
            (base_first, refs[groups], k * rows),
            (base_second, refs[groups + 1], k * rows),
        ):
            store(pl.multiple_of(base + s * blocks, SUB), ref, start)
    at_end = (lax.axis_index("dom") == 0) | (lax.axis_index("dom") == lax.axis_size("dom") - 1)

    @pl.when(at_end)
    def _():
        rows = pl.ds(pl.multiple_of(base_second, SUB), slab)
        region[rows, :] = jnp.zeros((slab, region.shape[1]), jnp.float32)

    clear_tail(region, 3 * slab)


def clear_tail(ref, first):
    if ref.shape[0] > first:
        ref[first:, :] = jnp.zeros((ref.shape[0] - first, ref.shape[1]), jnp.float32)


def parts_of(value):
    high = value.astype(jnp.bfloat16)
    rest = value - high.astype(jnp.float32)
    mid = rest.astype(jnp.bfloat16)
    return high, mid, (rest - mid.astype(jnp.float32)).astype(jnp.bfloat16)


def select(onehot, parts):
    total = None
    for part in reversed(parts):
        term = jnp.dot(onehot, part, preferred_element_type=jnp.float32)
        total = term if total is None else total + term
    return total


def far_fields(left, right, store):
    low = lane_iota(left.shape[0]) < HALF
    for n in range(left.shape[1] // LANES):
        one, two = left[:, n * LANES : (n + 1) * LANES], right[:, n * LANES : (n + 1) * LANES]
        store(2 * n, jnp.where(low, one, pltpu.roll(two, HALF, axis=1)))
        store(2 * n + 1, jnp.where(low, pltpu.roll(one, HALF, axis=1), two))


def column(value, index):
    at = index * SUB
    return jnp.broadcast_to(value[:, at : at + 1], (SUB, LANES))


def group_rows(g):
    return slice(g * SUB, (g + 1) * SUB)


def far_row(ref, field, tiles, d, t):
    return jnp.broadcast_to(ref[pl.ds((field * tiles + t) * SUB + d, 1), :], (SUB, LANES))


def each_slot(first, count, blocks, width, cols, result, group):
    together = 2 if count % 2 == 0 else 1
    lane = lane_iota()

    def body(step, carry):
        found = [[] for _ in range(width // SUB)]
        for n in range(together):
            d = step * together + n
            at = first + d
            own = pltpu.roll(cols[...], lax.rem(LANES - at, LANES), axis=1)
            for g in range(width // SUB):
                for m, value in enumerate(group(d, at, g, own[group_rows(g), :])):
                    found[g].append((m * blocks + at, jnp.sum(value, axis=1, keepdims=True)))
        for g in range(width // SUB):
            if found[g]:
                rows = result[group_rows(g), :]
                for at, total in found[g]:
                    rows = jnp.where(lane == at, total, rows)
                result[group_rows(g), :] = rows
        return carry

    lax.fori_loop(0, count // together, body, 0)


def sums_of(result, n, blocks, width):
    return jnp.transpose(result[...])[n * blocks : (n + 1) * blocks, 0:width]


def density_body(groups, blocks, width, tiles, *refs):
    parts = refs[: groups + 2]
    vol_out, rho_out, far, cols, own_rows, meta, hot, dist_out = refs[groups + 2 : groups + 10]
    region, own_range, own_tiles, result = refs[groups + 10 :]
    slab = groups * blocks
    me = lax.axis_index("seg")
    kept = parts[groups].shape[0] // groups

    def store(at, ref, start):
        rows = pl.ds(at, SUB)
        for n in range(4):
            region[rows, n * LANES : (n + 1) * LANES] = ref[start + n * SUB : start + (n + 1) * SUB, :]
        meta[rows, :] = ref[start + 4 * SUB : start + 5 * SUB, :]

    place_region(groups, blocks, parts, kept, region, store)
    clear_tail(meta, 3 * slab)
    for k in range(groups):
        rows = pl.ds(pl.multiple_of(jnp.bitwise_xor(me, k) * blocks, SUB), SUB)
        for n in range(6):
            own_range[rows, n * LANES : (n + 1) * LANES] = parts[k][n * SUB : (n + 1) * SUB, :]
    own_tiles[...] = jnp.zeros_like(own_tiles)
    result[...] = jnp.zeros_like(result)
    places = own_range[:, 4 * LANES + 2 * tiles : 4 * LANES + 2 * tiles + 1].astype(jnp.int32)
    wanted = me * blocks + lane_iota(slab)
    picks = jnp.where(jnp.broadcast_to(places, (slab, LANES)) == wanted, 1.0, 0.0)
    if slab < LANES:
        picks = jnp.concatenate([picks, jnp.zeros((LANES - slab, LANES), jnp.float32)], axis=0)
    picks = jnp.transpose(picks)[0:blocks, 0:slab].astype(jnp.bfloat16)
    mine = select(picks, parts_of(own_range[...]))
    entries = mine[:, 4 * LANES : 5 * LANES]
    for n in range(6):
        tile = mine[:, n * LANES : (n + 1) * LANES]
        if n == 4:
            continue
        at = 2 * n if n < 4 else 8
        own_rows[at] = tile
        own_rows[at + 1] = pltpu.roll(tile, HALF, axis=1)
    own_rows[10] = jnp.broadcast_to(entries[:, 2 * tiles + 1 : 2 * tiles + 2], (SUB, LANES))
    for n in range(8):
        own_tiles[n * SUB : (n + 1) * SUB, :] = own_rows[n]
    cols[...] = jnp.transpose(own_tiles[...])[0:width, :]
    size = region.shape[0]
    column_ids = lax.broadcasted_iota(jnp.int32, (SUB, size), 1)
    index = entries.astype(jnp.int32)
    for n in range(2 * tiles):
        chosen = jnp.broadcast_to(index[:, n : n + 1], (SUB, size)) == column_ids
        hot[n * SUB : (n + 1) * SUB, :] = jnp.where(chosen, 1.0, 0.0)
    values = parts_of(region[...])
    half = tiles * SUB
    left = select(hot[0:half, :].astype(jnp.bfloat16), values)
    right = select(hot[half:, :].astype(jnp.bfloat16), values)

    def keep(n, value):
        far[n * half : (n + 1) * half, :] = value

    far_fields(left, right, keep)

    def group(d, at, g, own):
        pos = [column(own, X + a) for a in range(3)]
        scale = 0.5 / column(own, SMOOTH)
        total = jnp.zeros((SUB, LANES), jnp.float32)
        for t in range(tiles):
            dx, dy, dz = [pos[a] - far_row(far, X + a, tiles, d, t) for a in range(3)]
            square = dx * dx + dy * dy + dz * dz
            dist = square * lax.rsqrt(jnp.maximum(square, TINY))
            dist_out[d, g, t] = dist
            ratio = dist * scale
            shell = jnp.maximum(1.0 - ratio, 0.0)
            shell = shell * shell
            shell = shell * shell
            total += shell * (far_row(far, MASS, tiles, d, t) * (0.25 + ratio))
        return [total]

    each_slot(0, blocks, blocks, width, cols, result, group)
    sums = sums_of(result, 0, blocks, width)
    smooth, mass, count = [own_rows[n, :, 0:width] for n in (SMOOTH, MASS, 10)]
    live = jnp.where(lane_iota()[:, 0:width].astype(jnp.float32) < count, 1.0, 0.0)
    rho = 4.0 * SIGMA / (smooth * smooth * smooth) * sums + (1.0 - live)
    rho_out[...] = rho
    vol = mass / rho
    vol_out[...] = jnp.concatenate([vol, vol], axis=1)


def placed_lists(slab, tiles, meta, hot):
    size = hot.shape[1]
    spot = meta[:, 2 * tiles : 2 * tiles + 1].astype(jnp.int32)
    rows = lax.broadcasted_iota(jnp.int32, (size, size), 0)
    start = jnp.where(rows < slab, 0, jnp.where(rows < 2 * slab, slab, 2 * slab))
    chosen = start + spot == lax.broadcasted_iota(jnp.int32, (size, size), 1)
    moves = jnp.where(chosen, 1.0, 0.0).astype(jnp.bfloat16)
    return jnp.dot(hot[...].astype(jnp.bfloat16), moves, preferred_element_type=jnp.float32)


def factor_body(first, count, blocks, slab, width, tiles, *refs):
    far, cols, dist = refs[:3]
    if first == 0:
        meta, hot = refs[3:5]
        refs[-1][...] = placed_lists(slab, tiles, meta, hot)
        slopes, products = refs[5:7]
    else:
        slopes, products = refs[3:5]

    def group(d, at, g, own):
        pos = [column(own, X + a) for a in range(3)]
        smooth = column(own, SMOOTH)
        for t in range(tiles):
            dx, dy, dz = [pos[a] - far_row(far, X + a, tiles, at, t) for a in range(3)]
            inv = 1.0 / (smooth + far_row(far, SMOOTH, tiles, at, t))
            inv2 = inv * inv
            part = jnp.maximum(inv - dist[at, g, t] * inv2, 0.0)
            weight = part * part * part * inv2
            ex, ey, ez = weight * dx, weight * dy, weight * dz
            slopes[0, d, g, t], slopes[1, d, g, t], slopes[2, d, g, t] = ex, ey, ez
            for n, term in enumerate((ex * dx, ey * dy, ez * dz, ex * dy, ex * dz, ey * dz)):
                products[n, d, g, t] = term
        return []

    each_slot(first, count, blocks, width, cols, None, group)


def tensor_body(spans, groups, blocks, width, tiles, *refs):
    cols, own_rows, hot, rho = refs[:4]
    products, refs = refs[4 : 4 + len(spans)], refs[4 + len(spans) :]
    vols = refs[: 2 + groups]
    coef_out, corr_out = refs[2 + groups : 4 + groups]
    region, far_vol, result = refs[4 + groups :]

    def store(at, ref, start):
        region[pl.ds(at, SUB), :] = ref[start : start + SUB, :]

    place_region(groups, blocks, vols, SUB, region, store)
    result[...] = jnp.zeros_like(result)
    values = parts_of(region[...])
    half = tiles * SUB
    left = select(hot[0:half, :].astype(jnp.bfloat16), values)
    right = select(hot[half:, :].astype(jnp.bfloat16), values)
    far_vol[...] = jnp.where(lane_iota(half) < HALF, left, right)

    def group(product, d, at, g, own):
        total = [jnp.zeros((SUB, LANES), jnp.float32) for _ in range(6)]
        for t in range(tiles):
            weight = far_row(far_vol, 0, tiles, at, t)
            for n in range(6):
                total[n] += product[n, d, g, t] * weight
        return total

    for (first, count), product in zip(spans, products):
        each_slot(first, count, blocks, width, cols, result, functools.partial(group, product))
    sums = jnp.transpose(result[...])
    press = GAMMA_LESS * own_rows[8, :, 0:width] / rho[...]
    scale = own_rows[MASS, :, 0:width] * press
    coefs = []
    for n in range(6):
        tensor = SLOPE * sums[n * blocks : (n + 1) * blocks, 0:width]
        corr = (2.0 + tensor) if n < 3 else tensor
        corr_out[n] = corr
        coefs.append(scale * corr)
    corr_out[6] = press
    for n in range(3):
        coef_out[n * SUB : (n + 1) * SUB, :] = jnp.concatenate(coefs[2 * n : 2 * n + 2], axis=1)


def moment_body(blocks, width, tiles, spans, far, cols, *refs):
    slopes, out, result = refs[: len(spans)], refs[-2], refs[-1]
    result[...] = jnp.zeros_like(result)

    def group(slope, start, d, at, g, own):
        vel = [column(own, VEL + a) for a in range(3)]
        total = [jnp.zeros((SUB, LANES), jnp.float32) for _ in range(9)]
        for t in range(tiles):
            mass = far_row(far, MASS, tiles, at, t)
            px, py, pz = [mass * slope[a, at - start, g, t] for a in range(3)]
            vx, vy, vz = [vel[a] - far_row(far, VEL + a, tiles, at, t) for a in range(3)]
            terms = (
                px,
                py,
                pz,
                vx * px,
                vy * py,
                vz * pz,
                vx * py + vy * px,
                vx * pz + vz * px,
                vy * pz + vz * py,
            )
            for n, term in enumerate(terms):
                total[n] += term
        return total

    for (low, count, start), slope in zip(spans, slopes):
        each_slot(low, count, blocks, width, cols, result, functools.partial(group, slope, start))
    sums = jnp.transpose(result[...])
    for n in range(9):
        out[n] = sums[n * blocks : (n + 1) * blocks, 0:width]


def update_body(spans, moment_count, groups, blocks, width, tiles, *refs):
    cols, own_rows, hot, corr = refs[:4]
    slopes, refs = refs[4 : 4 + len(spans)], refs[4 + len(spans) :]
    pieces, refs = refs[:moment_count], refs[moment_count:]
    coefs = refs[: 2 + groups]
    state_out = refs[2 + groups]
    region, far_coef, result = refs[3 + groups :]

    def store(at, ref, start):
        for n in range(3):
            tile = ref[start + n * SUB : start + (n + 1) * SUB, :]
            region[pl.ds(at, SUB), n * LANES : (n + 1) * LANES] = tile

    place_region(groups, blocks, coefs, 3 * SUB, region, store)
    result[...] = jnp.zeros_like(result)
    values = parts_of(region[...])
    half = tiles * SUB
    left = select(hot[0:half, :].astype(jnp.bfloat16), values)
    right = select(hot[half:, :].astype(jnp.bfloat16), values)

    def keep(n, value):
        far_coef[n * half : (n + 1) * half, :] = value

    far_fields(left, right, keep)

    def group(slope, d, at, g, own):
        total = [jnp.zeros((SUB, LANES), jnp.float32) for _ in range(3)]
        for t in range(tiles):
            ex, ey, ez = [slope[a, d, g, t] for a in range(3)]
            xx, yy, zz, xy, xz, yz = [far_row(far_coef, n, tiles, at, t) for n in range(6)]
            total[0] += xx * ex + xy * ey + xz * ez
            total[1] += xy * ex + yy * ey + yz * ez
            total[2] += xz * ex + yz * ey + zz * ez
        return total

    for (first, count), slope in zip(spans, slopes):
        each_slot(first, count, blocks, width, cols, result, functools.partial(group, slope))
    moments = [sum(piece[m] for piece in pieces) for m in range(9)]
    sums = jnp.transpose(result[...])
    field = lambda n: own_rows[n, :, 0:width]
    live = jnp.where(lane_iota()[:, 0:width].astype(jnp.float32) < field(10), 1.0, 0.0)
    press = corr[6]
    xx, yy, zz, xy, xz, yz = [corr[n] for n in range(6)]
    sx, sy, sz = [moments[n] for n in range(3)]
    near = (xx * sx + xy * sy + xz * sz, xy * sx + yy * sy + yz * sz, xz * sx + yz * sy + zz * sz)
    for a in range(3):
        far_sum = sums[a * blocks : (a + 1) * blocks, 0:width]
        accel = -SLOPE * live * (press * near[a] + far_sum)
        velocity = field(VEL + a) + STEP_DT * accel
        state_out[3 + a] = velocity
        state_out[a] = field(X + a) + STEP_DT * velocity
    heat = moments[3] * xx + moments[4] * yy + moments[5] * zz
    heat += moments[6] * xy + moments[7] * xz + moments[8] * yz
    state_out[6] = field(9)
    state_out[7] = field(SMOOTH)
    state_out[8] = field(8) + STEP_DT * (SLOPE * live * press * heat)


def exchange(own, send_rows):
    groups = lax.axis_size("seg")
    ranges = lax.axis_size("dom")
    seg = [own]
    for k in range(1, groups):
        seg.append(lax.ppermute(own, "seg", [(i, i ^ k) for i in range(groups)]))
    whole = jnp.concatenate([part[:send_rows] for part in seg], axis=0)
    first = [(i, i ^ 1) for i in range(ranges)]
    second = []
    for r in range(ranges):
        for s in range(groups):
            inside = 0 < r < ranges - 1
            other = (((r + 1) ^ 1) - 1) * groups + s if inside else r * groups + (s ^ 1)
            second.append((r * groups + s, other))
    return seg + [lax.ppermute(whole, "dom", first), lax.ppermute(whole, ("dom", "seg"), second)]


def spans_of(blocks, split):
    ends = [blocks * n // SUB for n in (0,) + split]
    return [(low, high - low) for low, high in zip(ends, ends[1:])]


def step(state, counts, neighbours, new_place):
    blocks, fields, width = state.shape
    nbr = neighbours.shape[1]
    groups = lax.axis_size("seg")
    slab = blocks * groups
    tiles = (nbr + 2) // 2
    size = -(-3 * slab // LANES) * LANES
    many = (blocks, width // SUB, tiles, SUB, LANES)
    f32, i32 = jnp.float32, jnp.int32
    vm = pl.BlockSpec(memory_space=VMEM)
    any_space = pl.BlockSpec(memory_space=pltpu.HBM)
    columns = VMEM((width, LANES), f32)
    packed = call(
        functools.partial(pack_body, blocks, width, nbr, tiles),
        shape(6 * SUB, LANES),
        in_specs=[any_space] * 4,
        out_specs=vm,
        scratch=(
            VMEM((fields, blocks, width), f32),
            VMEM((blocks, nbr), i32),
            SMEM((blocks,), i32),
            SMEM((blocks,), i32),
            pltpu.SemaphoreType.DMA((4,)),
        ),
    )(*[
        pltpu.with_memory_space_constraint(value, pltpu.HBM)
        for value in (counts, new_place, jnp.swapaxes(state, 0, 1), neighbours)
    ])
    parts = exchange(packed, 5 * SUB)
    vol, rho, far, cols, own_rows, meta, hot, dist = call(
        functools.partial(density_body, groups, blocks, width, tiles),
        (
            shape(SUB, LANES),
            shape(blocks, width),
            shape(8 * tiles * SUB, LANES),
            shape(width, LANES),
            shape(11, SUB, LANES),
            shape(size, LANES),
            shape(2 * tiles * SUB, size),
            shape(*many),
        ),
        in_specs=[vm] * (groups + 2),
        out_specs=(vm,) * 8,
        scratch=(
            VMEM((size, 4 * LANES), f32),
            VMEM((slab, 6 * LANES), f32),
            VMEM((LANES, LANES), f32),
            columns,
        ),
    )(*parts)
    vols = exchange(vol, SUB)
    spans = spans_of(blocks, FACTOR_SPLIT)
    slopes, products = [], []
    for n, (low, count) in enumerate(spans):
        outs = (shape(3, count, *many[1:]), shape(6, count, *many[1:]))
        extra = (meta, hot) if n == 0 else ()
        if n == 0:
            outs += (shape(2 * tiles * SUB, size),)
        found = call(
            functools.partial(factor_body, low, count, blocks, slab, width, tiles),
            outs,
            in_specs=[vm] * (3 + len(extra)),
            out_specs=(vm,) * len(outs),
        )(far, cols, dist, *extra)
        slopes.append(found[0])
        products.append(found[1])
        if n == 0:
            placed = found[2]
    coef, corr = call(
        functools.partial(tensor_body, spans, groups, blocks, width, tiles),
        (shape(3 * SUB, LANES), shape(7, blocks, width)),
        in_specs=[vm] * (4 + len(spans) + groups + 2),
        out_specs=(vm, vm),
        scratch=(VMEM((size, LANES), f32), VMEM((tiles * SUB, LANES), f32), columns),
    )(cols, own_rows, placed, rho, *products, *vols)
    coefs = exchange(coef, 3 * SUB)
    moments = []
    for low, count in spans_of(blocks, MOMENT_SPLIT):
        parts, used = [], []
        for (start, length), slope in zip(spans, slopes):
            begin, end = max(low, start), min(low + count, start + length)
            if begin < end:
                parts.append((begin, end - begin, start))
                used.append(slope)
        moments.append(
            call(
                functools.partial(moment_body, blocks, width, tiles, parts),
                shape(9, blocks, width),
                in_specs=[vm] * (2 + len(used)),
                out_specs=vm,
                scratch=(columns,),
            )(far, cols, *used)
        )
    moved = call(
        functools.partial(update_body, spans, len(moments), groups, blocks, width, tiles),
        shape(fields, blocks, width),
        in_specs=[vm] * (4 + len(spans) + len(moments) + groups + 2),
        out_specs=vm,
        scratch=(
            VMEM((size, 3 * LANES), f32),
            VMEM((6 * tiles * SUB, LANES), f32),
            columns,
        ),
    )(cols, own_rows, placed, corr, *slopes, *moments, *coefs)
    return (jnp.swapaxes(moved, 0, 1), rho)


def solution(mesh):
    return jax.shard_map(
        step,
        mesh=mesh,
        in_specs=(
            P(("dom", "seg"), None, None),
            P(("dom", "seg")),
            P(("dom", "seg"), None),
            P(("dom", "seg")),
        ),
        out_specs=(P(("dom", "seg"), None, None), P(("dom", "seg"), None)),
        check_vma=False,
    )
```

```python
import functools
import math

import jax
import jax.numpy as jnp
from jax import lax
from jax.experimental import pallas as pl
from jax.experimental.pallas import tpu as pltpu
from jax.sharding import PartitionSpec as P


SIGMA = 21.0 / (16.0 * math.pi)
GAMMA_LESS = 2.0 / 3.0
STEP_DT = 0.1
SLOPE = -5.0 * SIGMA * 32.0
TINY = 1e-37
FACTOR_SPLIT = (5, 8)
MOMENT_SPLIT = (4, 8)
SUB = 8
LANES = 128
X, SMOOTH, MASS, VEL = 0, 3, 4, 5
HALF = LANES // 2
VMEM = pltpu.VMEM
SMEM = pltpu.SMEM


def lane_iota(rows=SUB):
    return lax.broadcasted_iota(jnp.int32, (rows, LANES), 1)


def row_iota(rows=SUB):
    return lax.broadcasted_iota(jnp.int32, (rows, LANES), 0)


def call(body, outs, scratch=(), in_specs=None, out_specs=None, grant=8):
    return pl.pallas_call(
        body,
        out_shape=outs,
        in_specs=in_specs,
        out_specs=out_specs,
        scratch_shapes=list(scratch),
        compiler_params=pltpu.CompilerParams(vmem_limit_bytes=grant << 20),
    )


def shape(*dims, dtype=jnp.float32):
    return jax.ShapeDtypeStruct(dims, dtype)


def pack_body(blocks, width, nbr, tiles, *refs):
    counts, place, state, lists, out, held, entries, few, ids, sem = refs
    copies = [
        pltpu.make_async_copy(source, target, sem.at[n])
        for n, (source, target) in enumerate(
            ((state, held), (lists, entries), (counts, few), (place, ids))
        )
    ]
    for copy in copies:
        copy.start()
    for copy in copies:
        copy.wait()
    groups = lax.axis_size("seg")
    me = lax.axis_index("seg")
    lane, row = lane_iota(), row_iota()
    count = jnp.zeros((SUB, LANES), jnp.int32)
    spot = jnp.zeros((SUB, LANES), jnp.int32)
    for b in range(blocks):
        count = jnp.where(row == b, few[b], count)
        spot = jnp.where(row == b, ids[b], spot)
    listed = jnp.concatenate(
        [entries[...], jnp.zeros((blocks, LANES - nbr), jnp.int32)], axis=1
    ).astype(jnp.float32)
    listed = pltpu.roll(listed, 1, axis=1)
    own = (groups * blocks + me * blocks + row).astype(jnp.float32)
    meta = jnp.where(lane == 0, own, jnp.where(lane <= nbr, listed, -1.0))
    meta = jnp.where(lane == 2 * tiles, spot.astype(jnp.float32), meta)
    meta = jnp.where(lane == 2 * tiles + 1, count.astype(jnp.float32), meta)
    rows = [held[n] for n in range(9)]
    mass = jnp.where(lane[:, 0:width] < count[:, 0:width], rows[6], 0.0)
    order = (rows[0], rows[1], rows[2], rows[7], mass, rows[3], rows[4], rows[5])
    for n in range(4):
        out[n * SUB : (n + 1) * SUB, :] = jnp.concatenate(order[2 * n : 2 * n + 2], axis=1)
    out[4 * SUB : 5 * SUB, :] = meta
    out[5 * SUB : 6 * SUB, :] = jnp.concatenate([rows[8], rows[6]], axis=1)


def place_region(groups, blocks, refs, rows, region, store):
    slab = groups * blocks
    me = lax.axis_index("seg")
    odd = lax.rem(lax.axis_index("dom"), 2)
    base_first = jnp.where(odd == 0, 2 * slab, 0)
    base_second = jnp.where(odd == 0, 0, 2 * slab)
    for k in range(groups):
        s = jnp.bitwise_xor(me, k)
        for base, ref, start in (
            (slab, refs[k], 0),
            (base_first, refs[groups], k * rows),
            (base_second, refs[groups + 1], k * rows),
        ):
            store(pl.multiple_of(base + s * blocks, SUB), ref, start)
    at_end = (lax.axis_index("dom") == 0) | (lax.axis_index("dom") == lax.axis_size("dom") - 1)

    @pl.when(at_end)
    def _():
        rows = pl.ds(pl.multiple_of(base_second, SUB), slab)
        region[rows, :] = jnp.zeros((slab, region.shape[1]), jnp.float32)

    clear_tail(region, 3 * slab)


def clear_tail(ref, first):
    if ref.shape[0] > first:
        ref[first:, :] = jnp.zeros((ref.shape[0] - first, ref.shape[1]), jnp.float32)


def parts_of(value):
    high = value.astype(jnp.bfloat16)
    rest = value - high.astype(jnp.float32)
    mid = rest.astype(jnp.bfloat16)
    return high, mid, (rest - mid.astype(jnp.float32)).astype(jnp.bfloat16)


def select(onehot, parts):
    total = None
    for part in reversed(parts):
        term = jnp.dot(onehot, part, preferred_element_type=jnp.float32)
        total = term if total is None else total + term
    return total


def far_fields(left, right, store):
    low = lane_iota(left.shape[0]) < HALF
    for n in range(left.shape[1] // LANES):
        one, two = left[:, n * LANES : (n + 1) * LANES], right[:, n * LANES : (n + 1) * LANES]
        store(2 * n, jnp.where(low, one, pltpu.roll(two, HALF, axis=1)))
        store(2 * n + 1, jnp.where(low, pltpu.roll(one, HALF, axis=1), two))


def column(value, index):
    at = index * SUB
    return jnp.broadcast_to(value[:, at : at + 1], (SUB, LANES))


def group_rows(g):
    return slice(g * SUB, (g + 1) * SUB)


def far_row(ref, field, tiles, d, t):
    return jnp.broadcast_to(ref[pl.ds((field * tiles + t) * SUB + d, 1), :], (SUB, LANES))


def each_slot(first, count, blocks, width, cols, result, group, together=2):
    lane = lane_iota()

    def body(start, together):
        found = [[] for _ in range(width // SUB)]
        for n in range(together):
            d = start + n
            at = first + d
            own = pltpu.roll(cols[...], lax.rem(LANES - at, LANES), axis=1)
            for g in range(width // SUB):
                for m, value in enumerate(group(d, at, g, own[group_rows(g), :])):
                    found[g].append((m * blocks + at, jnp.sum(value, axis=1, keepdims=True)))
        for g in range(width // SUB):
            if found[g]:
                rows = result[group_rows(g), :]
                for at, total in found[g]:
                    rows = jnp.where(lane == at, total, rows)
                result[group_rows(g), :] = rows

    def step(i, carry):
        body(i * together, together)
        return carry

    lax.fori_loop(0, count // together, step, 0)
    if count % together:
        body(count - count % together, count % together)


def sums_of(result, n, blocks, width):
    return jnp.transpose(result[...])[n * blocks : (n + 1) * blocks, 0:width]


def lists_body(groups, blocks, width, tiles, *refs):
    parts = refs[:groups]
    cols, own_rows, hot, own_range, own_tiles = refs[groups:]
    slab = groups * blocks
    me = lax.axis_index("seg")
    for k in range(groups):
        rows = pl.ds(pl.multiple_of(jnp.bitwise_xor(me, k) * blocks, SUB), SUB)
        for n in range(6):
            own_range[rows, n * LANES : (n + 1) * LANES] = parts[k][n * SUB : (n + 1) * SUB, :]
    own_tiles[...] = jnp.zeros_like(own_tiles)
    places = own_range[:, 4 * LANES + 2 * tiles : 4 * LANES + 2 * tiles + 1].astype(jnp.int32)
    wanted = me * blocks + lane_iota(slab)
    picks = jnp.where(jnp.broadcast_to(places, (slab, LANES)) == wanted, 1.0, 0.0)
    if slab < LANES:
        picks = jnp.concatenate([picks, jnp.zeros((LANES - slab, LANES), jnp.float32)], axis=0)
    picks = jnp.transpose(picks)[0:blocks, 0:slab].astype(jnp.bfloat16)
    mine = select(picks, parts_of(own_range[...]))
    entries = mine[:, 4 * LANES : 5 * LANES]
    for n in range(6):
        tile = mine[:, n * LANES : (n + 1) * LANES]
        if n == 4:
            continue
        at = 2 * n if n < 4 else 8
        own_rows[at] = tile
        own_rows[at + 1] = pltpu.roll(tile, HALF, axis=1)
    own_rows[10] = jnp.broadcast_to(entries[:, 2 * tiles + 1 : 2 * tiles + 2], (SUB, LANES))
    for n in range(8):
        own_tiles[n * SUB : (n + 1) * SUB, :] = own_rows[n]
    cols[...] = jnp.transpose(own_tiles[...])[0:width, :]
    size = hot.shape[1]
    column_ids = lax.broadcasted_iota(jnp.int32, (SUB, size), 1)
    index = entries.astype(jnp.int32)
    for n in range(2 * tiles):
        chosen = jnp.broadcast_to(index[:, n : n + 1], (SUB, size)) == column_ids
        hot[n * SUB : (n + 1) * SUB, :] = jnp.where(chosen, 1.0, 0.0)


def density_body(groups, blocks, width, tiles, *refs):
    cols, own_rows, hot = refs[:3]
    parts = refs[3 : groups + 5]
    vol_out, rho_out, far, meta, dist_out, region, result = refs[groups + 5 :]
    slab = groups * blocks
    kept = parts[groups].shape[0] // groups

    def store(at, ref, start):
        rows = pl.ds(at, SUB)
        for n in range(4):
            region[rows, n * LANES : (n + 1) * LANES] = ref[start + n * SUB : start + (n + 1) * SUB, :]
        meta[rows, :] = ref[start + 4 * SUB : start + 5 * SUB, :]

    place_region(groups, blocks, parts, kept, region, store)
    clear_tail(meta, 3 * slab)
    result[...] = jnp.zeros_like(result)
    values = parts_of(region[...])
    half = tiles * SUB
    both = select(hot[...].astype(jnp.bfloat16), values)
    left, right = both[0:half], both[half:]

    def keep(n, value):
        far[n * half : (n + 1) * half, :] = value

    far_fields(left, right, keep)

    def group(d, at, g, own):
        pos = [column(own, X + a) for a in range(3)]
        scale = 0.5 / column(own, SMOOTH)
        total = jnp.zeros((SUB, LANES), jnp.float32)
        for t in range(tiles):
            dx, dy, dz = [pos[a] - far_row(far, X + a, tiles, d, t) for a in range(3)]
            square = dx * dx + dy * dy + dz * dz
            dist = square * lax.rsqrt(jnp.maximum(square, TINY))
            dist_out[d, g, t] = dist
            ratio = dist * scale
            shell = jnp.maximum(1.0 - ratio, 0.0)
            shell = shell * shell
            shell = shell * shell
            total += shell * (far_row(far, MASS, tiles, d, t) * (0.25 + ratio))
        return [total]

    each_slot(0, blocks, blocks, width, cols, result, group)
    sums = sums_of(result, 0, blocks, width)
    smooth, count = [own_rows[n, :, 0:width] for n in (SMOOTH, 10)]
    live = jnp.where(lane_iota()[:, 0:width].astype(jnp.float32) < count, 1.0, 0.0)
    rho = 4.0 * SIGMA / (smooth * smooth * smooth) * sums + (1.0 - live)
    rho_out[...] = rho
    share = 1.0 / rho
    vol_out[...] = jnp.concatenate([share, share], axis=1)


def placed_lists(slab, tiles, meta, hot):
    size = hot.shape[1]
    spot = meta[:, 2 * tiles : 2 * tiles + 1].astype(jnp.int32)
    rows = lax.broadcasted_iota(jnp.int32, (size, size), 0)
    start = jnp.where(rows < slab, 0, jnp.where(rows < 2 * slab, slab, 2 * slab))
    chosen = start + spot == lax.broadcasted_iota(jnp.int32, (size, size), 1)
    moves = jnp.where(chosen, 1.0, 0.0).astype(jnp.bfloat16)
    return jnp.dot(hot[...].astype(jnp.bfloat16), moves, preferred_element_type=jnp.float32)


def factor_body(first, count, blocks, slab, width, tiles, *refs):
    far, cols, dist = refs[:3]
    if first == 0:
        meta, hot = refs[3:5]
        refs[-1][...] = placed_lists(slab, tiles, meta, hot)
        slopes, products = refs[5:7]
    else:
        slopes, products = refs[3:5]

    def group(d, at, g, own):
        pos = [column(own, X + a) for a in range(3)]
        smooth = column(own, SMOOTH)
        for t in range(tiles):
            dx, dy, dz = [pos[a] - far_row(far, X + a, tiles, at, t) for a in range(3)]
            inv = 1.0 / (smooth + far_row(far, SMOOTH, tiles, at, t))
            inv2 = inv * inv
            part = jnp.maximum(inv - dist[at, g, t] * inv2, 0.0)
            weight = part * part * part * inv2 * far_row(far, MASS, tiles, at, t)
            ex, ey, ez = weight * dx, weight * dy, weight * dz
            slopes[0, d, g, t], slopes[1, d, g, t], slopes[2, d, g, t] = ex, ey, ez
            for n, term in enumerate((ex * dx, ey * dy, ez * dz, ex * dy, ex * dz, ey * dz)):
                products[n, d, g, t] = term
        return []

    each_slot(first, count, blocks, width, cols, None, group)


def tensor_body(spans, groups, blocks, width, tiles, *refs):
    cols, own_rows, hot, rho = refs[:4]
    products, refs = refs[4 : 4 + len(spans)], refs[4 + len(spans) :]
    vols = refs[: 2 + groups]
    coef_out, corr_out = refs[2 + groups : 4 + groups]
    region, far_vol, result = refs[4 + groups :]

    def store(at, ref, start):
        region[pl.ds(at, SUB), :] = ref[start : start + SUB, :]

    place_region(groups, blocks, vols, SUB, region, store)
    result[...] = jnp.zeros_like(result)
    values = parts_of(region[...])
    half = tiles * SUB
    both = select(hot[...].astype(jnp.bfloat16), values)
    left, right = both[0:half], both[half:]
    far_vol[...] = jnp.where(lane_iota(half) < HALF, left, right)

    def group(product, d, at, g, own):
        total = [jnp.zeros((SUB, LANES), jnp.float32) for _ in range(6)]
        for t in range(tiles):
            weight = far_row(far_vol, 0, tiles, at, t)
            for n in range(6):
                total[n] += product[n, d, g, t] * weight
        return total

    for (first, count), product in zip(spans, products):
        each_slot(first, count, blocks, width, cols, result, functools.partial(group, product))
    sums = jnp.transpose(result[...])
    press = GAMMA_LESS * own_rows[8, :, 0:width] / rho[...]
    coefs = []
    for n in range(6):
        tensor = SLOPE * sums[n * blocks : (n + 1) * blocks, 0:width]
        corr = (2.0 + tensor) if n < 3 else tensor
        corr_out[n] = corr
        coefs.append(press * corr)
    corr_out[6] = press
    for n in range(3):
        coef_out[n * SUB : (n + 1) * SUB, :] = jnp.concatenate(coefs[2 * n : 2 * n + 2], axis=1)


def moment_body(blocks, width, tiles, spans, far, cols, *refs):
    slopes, out, result = refs[: len(spans)], refs[-2], refs[-1]
    result[...] = jnp.zeros_like(result)

    def group(slope, start, d, at, g, own):
        vel = [column(own, VEL + a) for a in range(3)]
        total = [jnp.zeros((SUB, LANES), jnp.float32) for _ in range(9)]
        for t in range(tiles):
            px, py, pz = [slope[a, at - start, g, t] for a in range(3)]
            vx, vy, vz = [vel[a] - far_row(far, VEL + a, tiles, at, t) for a in range(3)]
            terms = (
                px,
                py,
                pz,
                vx * px,
                vy * py,
                vz * pz,
                vx * py + vy * px,
                vx * pz + vz * px,
                vy * pz + vz * py,
            )
            for n, term in enumerate(terms):
                total[n] += term
        return total

    for (low, count, start), slope in zip(spans, slopes):
        each_slot(low, count, blocks, width, cols, result, functools.partial(group, slope, start), 1)
    sums = jnp.transpose(result[...])
    for n in range(9):
        out[n] = sums[n * blocks : (n + 1) * blocks, 0:width]


def update_body(spans, moment_count, groups, blocks, width, tiles, *refs):
    cols, own_rows, hot, corr = refs[:4]
    slopes, refs = refs[4 : 4 + len(spans)], refs[4 + len(spans) :]
    pieces, refs = refs[:moment_count], refs[moment_count:]
    coefs = refs[: 2 + groups]
    state_out = refs[2 + groups]
    region, far_coef, result = refs[3 + groups :]

    def store(at, ref, start):
        for n in range(3):
            tile = ref[start + n * SUB : start + (n + 1) * SUB, :]
            region[pl.ds(at, SUB), n * LANES : (n + 1) * LANES] = tile

    place_region(groups, blocks, coefs, 3 * SUB, region, store)
    result[...] = jnp.zeros_like(result)
    values = parts_of(region[...])
    half = tiles * SUB
    both = select(hot[...].astype(jnp.bfloat16), values)
    left, right = both[0:half], both[half:]

    def keep(n, value):
        far_coef[n * half : (n + 1) * half, :] = value

    far_fields(left, right, keep)

    def group(slope, d, at, g, own):
        total = [jnp.zeros((SUB, LANES), jnp.float32) for _ in range(3)]
        for t in range(tiles):
            ex, ey, ez = [slope[a, d, g, t] for a in range(3)]
            xx, yy, zz, xy, xz, yz = [far_row(far_coef, n, tiles, at, t) for n in range(6)]
            total[0] += xx * ex + xy * ey + xz * ez
            total[1] += xy * ex + yy * ey + yz * ez
            total[2] += xz * ex + yz * ey + zz * ez
        return total

    for (first, count), slope in zip(spans, slopes):
        each_slot(first, count, blocks, width, cols, result, functools.partial(group, slope))
    moments = [sum(piece[m] for piece in pieces) for m in range(9)]
    sums = jnp.transpose(result[...])
    field = lambda n: own_rows[n, :, 0:width]
    live = jnp.where(lane_iota()[:, 0:width].astype(jnp.float32) < field(10), 1.0, 0.0)
    press = corr[6]
    xx, yy, zz, xy, xz, yz = [corr[n] for n in range(6)]
    sx, sy, sz = [moments[n] for n in range(3)]
    near = (xx * sx + xy * sy + xz * sz, xy * sx + yy * sy + yz * sz, xz * sx + yz * sy + zz * sz)
    for a in range(3):
        far_sum = sums[a * blocks : (a + 1) * blocks, 0:width]
        accel = -SLOPE * live * (press * near[a] + far_sum)
        velocity = field(VEL + a) + STEP_DT * accel
        state_out[3 + a] = velocity
        state_out[a] = field(X + a) + STEP_DT * velocity
    heat = moments[3] * xx + moments[4] * yy + moments[5] * zz
    heat += moments[6] * xy + moments[7] * xz + moments[8] * yz
    state_out[6] = field(9)
    state_out[7] = field(SMOOTH)
    state_out[8] = field(8) + STEP_DT * (SLOPE * live * press * heat)


def exchange(own, send_rows):
    groups = lax.axis_size("seg")
    ranges = lax.axis_size("dom")
    seg = [own]
    for k in range(1, groups):
        seg.append(lax.ppermute(own, "seg", [(i, i ^ k) for i in range(groups)]))
    whole = jnp.concatenate([part[:send_rows] for part in seg], axis=0)
    first = [(i, i ^ 1) for i in range(ranges)]
    second = []
    for r in range(ranges):
        for s in range(groups):
            inside = 0 < r < ranges - 1
            other = (((r + 1) ^ 1) - 1) * groups + s if inside else r * groups + (s ^ 1)
            second.append((r * groups + s, other))
    near = lax.ppermute(whole, "dom", first)
    beside = lax.ppermute(whole, ("dom", "seg"), second)
    return seg + [near, beside]


def spans_of(blocks, split):
    ends = [blocks * n // SUB for n in (0,) + split]
    return [(low, high - low) for low, high in zip(ends, ends[1:])]


def step(state, counts, neighbours, new_place):
    blocks, fields, width = state.shape
    nbr = neighbours.shape[1]
    groups = lax.axis_size("seg")
    slab = blocks * groups
    tiles = (nbr + 2) // 2
    size = -(-3 * slab // LANES) * LANES
    many = (blocks, width // SUB, tiles, SUB, LANES)
    f32, i32 = jnp.float32, jnp.int32
    vm = pl.BlockSpec(memory_space=VMEM)
    any_space = pl.BlockSpec(memory_space=pltpu.HBM)
    columns = VMEM((width, LANES), f32)
    packed = call(
        functools.partial(pack_body, blocks, width, nbr, tiles),
        shape(6 * SUB, LANES),
        in_specs=[any_space] * 4,
        out_specs=vm,
        scratch=(
            VMEM((fields, blocks, width), f32),
            VMEM((blocks, nbr), i32),
            SMEM((blocks,), i32),
            SMEM((blocks,), i32),
            pltpu.SemaphoreType.DMA((4,)),
        ),
    )(*[
        pltpu.with_memory_space_constraint(value, pltpu.HBM)
        for value in (counts, new_place, jnp.swapaxes(state, 0, 1), neighbours)
    ])
    parts = exchange(packed, 5 * SUB)
    cols, own_rows, hot = call(
        functools.partial(lists_body, groups, blocks, width, tiles),
        (
            shape(width, LANES),
            shape(11, SUB, LANES),
            shape(2 * tiles * SUB, size),
        ),
        in_specs=[vm] * groups,
        out_specs=(vm,) * 3,
        scratch=(VMEM((slab, 6 * LANES), f32), VMEM((LANES, LANES), f32)),
    )(*parts[:groups])
    vol, rho, far, meta, dist = call(
        functools.partial(density_body, groups, blocks, width, tiles),
        (
            shape(SUB, LANES),
            shape(blocks, width),
            shape(8 * tiles * SUB, LANES),
            shape(size, LANES),
            shape(*many),
        ),
        in_specs=[vm] * (groups + 5),
        out_specs=(vm,) * 5,
        scratch=(VMEM((size, 4 * LANES), f32), columns),
    )(cols, own_rows, hot, *parts)
    vols = exchange(vol, SUB)
    spans = spans_of(blocks, FACTOR_SPLIT)
    slopes, products = [], []
    for n, (low, count) in enumerate(spans):
        outs = (shape(3, count, *many[1:]), shape(6, count, *many[1:]))
        extra = (meta, hot) if n == 0 else ()
        if n == 0:
            outs += (shape(2 * tiles * SUB, size),)
        found = call(
            functools.partial(factor_body, low, count, blocks, slab, width, tiles),
            outs,
            in_specs=[vm] * (3 + len(extra)),
            out_specs=(vm,) * len(outs),
        )(far, cols, dist, *extra)
        slopes.append(found[0])
        products.append(found[1])
        if n == 0:
            placed = found[2]
    coef, corr = call(
        functools.partial(tensor_body, spans, groups, blocks, width, tiles),
        (shape(3 * SUB, LANES), shape(7, blocks, width)),
        in_specs=[vm] * (4 + len(spans) + groups + 2),
        out_specs=(vm, vm),
        scratch=(VMEM((size, LANES), f32), VMEM((tiles * SUB, LANES), f32), columns),
    )(cols, own_rows, placed, rho, *products, *vols)
    coefs = exchange(coef, 3 * SUB)
    moments = []
    for low, count in spans_of(blocks, MOMENT_SPLIT):
        parts, used = [], []
        for (start, length), slope in zip(spans, slopes):
            begin, end = max(low, start), min(low + count, start + length)
            if begin < end:
                parts.append((begin, end - begin, start))
                used.append(slope)
        moments.append(
            call(
                functools.partial(moment_body, blocks, width, tiles, parts),
                shape(9, blocks, width),
                in_specs=[vm] * (2 + len(used)),
                out_specs=vm,
                scratch=(columns,),
            )(far, cols, *used)
        )
    moved = call(
        functools.partial(update_body, spans, len(moments), groups, blocks, width, tiles),
        shape(fields, blocks, width),
        in_specs=[vm] * (4 + len(spans) + len(moments) + groups + 2),
        out_specs=vm,
        scratch=(
            VMEM((size, 3 * LANES), f32),
            VMEM((6 * tiles * SUB, LANES), f32),
            columns,
        ),
    )(cols, own_rows, placed, corr, *slopes, *moments, *coefs)
    return (jnp.swapaxes(moved, 0, 1), rho)


def solution(mesh):
    return jax.shard_map(
        step,
        mesh=mesh,
        in_specs=(
            P(("dom", "seg"), None, None),
            P(("dom", "seg")),
            P(("dom", "seg"), None),
            P(("dom", "seg")),
        ),
        out_specs=(P(("dom", "seg"), None, None), P(("dom", "seg"), None)),
        check_vma=False,
    )
```

```python
import functools
import math

import jax
import jax.numpy as jnp
from jax import lax
from jax.experimental import pallas as pl
from jax.experimental.pallas import tpu as pltpu
from jax.sharding import PartitionSpec as P


SIGMA = 21.0 / (16.0 * math.pi)
GAMMA_LESS = 2.0 / 3.0
STEP_DT = 0.1
SLOPE = -5.0 * SIGMA * 32.0
TINY = 1e-37
FACTOR_SPLIT = (5, 8)
MOMENT_SPLIT = (4, 8)
SUB = 8
LANES = 128
X, SMOOTH, MASS, VEL = 0, 3, 4, 5
HALF = LANES // 2
VMEM = pltpu.VMEM
SMEM = pltpu.SMEM


def lane_iota(rows=SUB):
    return lax.broadcasted_iota(jnp.int32, (rows, LANES), 1)


def row_iota(rows=SUB):
    return lax.broadcasted_iota(jnp.int32, (rows, LANES), 0)


def call(body, outs, scratch=(), in_specs=None, out_specs=None, grant=8):
    return pl.pallas_call(
        body,
        out_shape=outs,
        in_specs=in_specs,
        out_specs=out_specs,
        scratch_shapes=list(scratch),
        compiler_params=pltpu.CompilerParams(vmem_limit_bytes=grant << 20),
    )


def shape(*dims, dtype=jnp.float32):
    return jax.ShapeDtypeStruct(dims, dtype)


def pack_body(blocks, width, nbr, tiles, *refs):
    counts, place, state, lists, out, held, entries, few, ids, sem = refs
    copies = [
        pltpu.make_async_copy(source, target, sem.at[n])
        for n, (source, target) in enumerate(
            ((state, held), (lists, entries), (counts, few), (place, ids))
        )
    ]
    for copy in copies:
        copy.start()
    for copy in copies:
        copy.wait()
    groups = lax.axis_size("seg")
    me = lax.axis_index("seg")
    lane, row = lane_iota(), row_iota()
    count = jnp.zeros((SUB, LANES), jnp.int32)
    spot = jnp.zeros((SUB, LANES), jnp.int32)
    for b in range(blocks):
        count = jnp.where(row == b, few[b], count)
        spot = jnp.where(row == b, ids[b], spot)
    listed = jnp.concatenate(
        [entries[...], jnp.zeros((blocks, LANES - nbr), jnp.int32)], axis=1
    ).astype(jnp.float32)
    listed = pltpu.roll(listed, 1, axis=1)
    own = (groups * blocks + me * blocks + row).astype(jnp.float32)
    meta = jnp.where(lane == 0, own, jnp.where(lane <= nbr, listed, -1.0))
    meta = jnp.where(lane == 2 * tiles, spot.astype(jnp.float32), meta)
    meta = jnp.where(lane == 2 * tiles + 1, count.astype(jnp.float32), meta)
    rows = [held[n] for n in range(9)]
    mass = jnp.where(lane[:, 0:width] < count[:, 0:width], rows[6], 0.0)
    order = (rows[0], rows[1], rows[2], rows[7], mass, rows[3], rows[4], rows[5])
    for n in range(4):
        out[n * SUB : (n + 1) * SUB, :] = jnp.concatenate(order[2 * n : 2 * n + 2], axis=1)
    out[4 * SUB : 5 * SUB, :] = meta
    out[5 * SUB : 6 * SUB, :] = jnp.concatenate([rows[8], rows[6]], axis=1)


def place_region(groups, blocks, refs, rows, region, store):
    slab = groups * blocks
    me = lax.axis_index("seg")
    odd = lax.rem(lax.axis_index("dom"), 2)
    base_first = jnp.where(odd == 0, 2 * slab, 0)
    base_second = jnp.where(odd == 0, 0, 2 * slab)
    for k in range(groups):
        s = jnp.bitwise_xor(me, k)
        for base, ref, start in (
            (slab, refs[k], 0),
            (base_first, refs[groups], k * rows),
            (base_second, refs[groups + 1], k * rows),
        ):
            store(pl.multiple_of(base + s * blocks, SUB), ref, start)
    at_end = (lax.axis_index("dom") == 0) | (lax.axis_index("dom") == lax.axis_size("dom") - 1)

    @pl.when(at_end)
    def _():
        rows = pl.ds(pl.multiple_of(base_second, SUB), slab)
        region[rows, :] = jnp.zeros((slab, region.shape[1]), jnp.float32)

    clear_tail(region, 3 * slab)


def clear_tail(ref, first):
    if ref.shape[0] > first:
        ref[first:, :] = jnp.zeros((ref.shape[0] - first, ref.shape[1]), jnp.float32)


def parts_of(value):
    high = value.astype(jnp.bfloat16)
    rest = value - high.astype(jnp.float32)
    mid = rest.astype(jnp.bfloat16)
    return high, mid, (rest - mid.astype(jnp.float32)).astype(jnp.bfloat16)


def select(onehot, parts):
    total = None
    for part in reversed(parts):
        term = jnp.dot(onehot, part, preferred_element_type=jnp.float32)
        total = term if total is None else total + term
    return total


def far_fields(left, right, store):
    low = lane_iota(left.shape[0]) < HALF
    for n in range(left.shape[1] // LANES):
        one, two = left[:, n * LANES : (n + 1) * LANES], right[:, n * LANES : (n + 1) * LANES]
        store(2 * n, jnp.where(low, one, pltpu.roll(two, HALF, axis=1)))
        store(2 * n + 1, jnp.where(low, pltpu.roll(one, HALF, axis=1), two))


def column(value, index):
    at = index * SUB
    return jnp.broadcast_to(value[:, at : at + 1], (SUB, LANES))


def group_rows(g):
    return slice(g * SUB, (g + 1) * SUB)


def far_row(ref, field, tiles, d, t):
    return jnp.broadcast_to(ref[pl.ds((field * tiles + t) * SUB + d, 1), :], (SUB, LANES))


def each_slot(first, count, blocks, width, cols, result, group, together=2, batch=1):
    lane = lane_iota()

    def body(start, together):
        found = [[] for _ in range(width // SUB)]
        for n in range(together):
            d = start + n
            at = first + d
            own = pltpu.roll(cols[...], lax.rem(LANES - at, LANES), axis=1)
            for low in range(0, width // SUB, batch):
                rows = [own[group_rows(low + n), :] for n in range(batch)]
                if batch == 1:
                    values = [group(d, at, low, rows[0])]
                else:
                    values = group(d, at, low, rows)
                for n, totals in enumerate(values):
                    for m, value in enumerate(totals):
                        total = jnp.sum(value, axis=1, keepdims=True)
                        found[low + n].append((m * blocks + at, total))
        for g in range(width // SUB):
            if found[g]:
                rows = result[group_rows(g), :]
                for at, total in found[g]:
                    rows = jnp.where(lane == at, total, rows)
                result[group_rows(g), :] = rows

    def step(i, carry):
        body(i * together, together)
        return carry

    lax.fori_loop(0, count // together, step, 0)
    if count % together:
        body(count - count % together, count % together)


def sums_of(result, n, blocks, width):
    return jnp.transpose(result[...])[n * blocks : (n + 1) * blocks, 0:width]


def lists_body(groups, blocks, width, tiles, *refs):
    parts = refs[:groups]
    cols, own_rows, hot, own_range, own_tiles = refs[groups:]
    slab = groups * blocks
    me = lax.axis_index("seg")
    for k in range(groups):
        rows = pl.ds(pl.multiple_of(jnp.bitwise_xor(me, k) * blocks, SUB), SUB)
        for n in range(6):
            own_range[rows, n * LANES : (n + 1) * LANES] = parts[k][n * SUB : (n + 1) * SUB, :]
    own_tiles[...] = jnp.zeros_like(own_tiles)
    places = own_range[:, 4 * LANES + 2 * tiles : 4 * LANES + 2 * tiles + 1].astype(jnp.int32)
    wanted = me * blocks + lane_iota(slab)
    picks = jnp.where(jnp.broadcast_to(places, (slab, LANES)) == wanted, 1.0, 0.0)
    if slab < LANES:
        picks = jnp.concatenate([picks, jnp.zeros((LANES - slab, LANES), jnp.float32)], axis=0)
    picks = jnp.transpose(picks)[0:blocks, 0:slab].astype(jnp.bfloat16)
    mine = select(picks, parts_of(own_range[...]))
    entries = mine[:, 4 * LANES : 5 * LANES]
    for n in range(6):
        tile = mine[:, n * LANES : (n + 1) * LANES]
        if n == 4:
            continue
        at = 2 * n if n < 4 else 8
        own_rows[at] = tile
        own_rows[at + 1] = pltpu.roll(tile, HALF, axis=1)
    own_rows[10] = jnp.broadcast_to(entries[:, 2 * tiles + 1 : 2 * tiles + 2], (SUB, LANES))
    for n in range(8):
        own_tiles[n * SUB : (n + 1) * SUB, :] = own_rows[n]
    cols[...] = jnp.transpose(own_tiles[...])[0:width, :]
    size = hot.shape[1]
    column_ids = lax.broadcasted_iota(jnp.int32, (SUB, size), 1)
    index = entries.astype(jnp.int32)
    for n in range(2 * tiles):
        chosen = jnp.broadcast_to(index[:, n : n + 1], (SUB, size)) == column_ids
        hot[n * SUB : (n + 1) * SUB, :] = jnp.where(chosen, 1.0, 0.0)


def density_body(groups, blocks, width, tiles, *refs):
    cols, own_rows, hot = refs[:3]
    parts = refs[3 : groups + 5]
    vol_out, rho_out, far, meta, dist_out, region, result = refs[groups + 5 :]
    slab = groups * blocks
    kept = parts[groups].shape[0] // groups

    def store(at, ref, start):
        rows = pl.ds(at, SUB)
        for n in range(4):
            region[rows, n * LANES : (n + 1) * LANES] = ref[start + n * SUB : start + (n + 1) * SUB, :]
        meta[rows, :] = ref[start + 4 * SUB : start + 5 * SUB, :]

    place_region(groups, blocks, parts, kept, region, store)
    clear_tail(meta, 3 * slab)
    result[...] = jnp.zeros_like(result)
    values = parts_of(region[...])
    half = tiles * SUB
    both = select(hot[...].astype(jnp.bfloat16), values)
    left, right = both[0:half], both[half:]

    def keep(n, value):
        far[n * half : (n + 1) * half, :] = value

    far_fields(left, right, keep)

    def group(d, at, low, owns):
        pos = [[column(own, X + a) for a in range(3)] for own in owns]
        scale = [0.5 / column(own, SMOOTH) for own in owns]
        total = [jnp.zeros((SUB, LANES), jnp.float32) for _ in owns]
        for t in range(tiles):
            far_pos = [far_row(far, X + a, tiles, at, t) for a in range(3)]
            mass = far_row(far, MASS, tiles, at, t)
            for n in range(len(owns)):
                dx, dy, dz = [pos[n][a] - far_pos[a] for a in range(3)]
                square = dx * dx + dy * dy + dz * dz
                dist = square * lax.rsqrt(jnp.maximum(square, TINY))
                dist_out[at, low + n, t] = dist
                ratio = dist * scale[n]
                shell = jnp.maximum(1.0 - ratio, 0.0)
                shell = shell * shell
                shell = shell * shell
                total[n] += shell * (mass * (0.25 + ratio))
        return [[value] for value in total]

    each_slot(0, blocks, blocks, width, cols, result, group, 2, 4)
    sums = sums_of(result, 0, blocks, width)
    smooth, count = [own_rows[n, :, 0:width] for n in (SMOOTH, 10)]
    live = jnp.where(lane_iota()[:, 0:width].astype(jnp.float32) < count, 1.0, 0.0)
    rho = 4.0 * SIGMA / (smooth * smooth * smooth) * sums + (1.0 - live)
    rho_out[...] = rho
    share = 1.0 / rho
    vol_out[...] = jnp.concatenate([share, share], axis=1)


def placed_lists(slab, tiles, meta, hot):
    size = hot.shape[1]
    spot = meta[:, 2 * tiles : 2 * tiles + 1].astype(jnp.int32)
    rows = lax.broadcasted_iota(jnp.int32, (size, size), 0)
    start = jnp.where(rows < slab, 0, jnp.where(rows < 2 * slab, slab, 2 * slab))
    chosen = start + spot == lax.broadcasted_iota(jnp.int32, (size, size), 1)
    moves = jnp.where(chosen, 1.0, 0.0).astype(jnp.bfloat16)
    return jnp.dot(hot[...].astype(jnp.bfloat16), moves, preferred_element_type=jnp.float32)


def factor_body(first, count, blocks, slab, width, tiles, *refs):
    far, cols, dist = refs[:3]
    if first == 0:
        meta, hot = refs[3:5]
        refs[-1][...] = placed_lists(slab, tiles, meta, hot)
        slopes, products = refs[5:7]
    else:
        slopes, products = refs[3:5]

    def group(d, at, low, owns):
        pos = [[column(own, X + a) for a in range(3)] for own in owns]
        smooth = [column(own, SMOOTH) for own in owns]
        for t in range(tiles):
            far_pos = [far_row(far, X + a, tiles, at, t) for a in range(3)]
            far_smooth = far_row(far, SMOOTH, tiles, at, t)
            mass = far_row(far, MASS, tiles, at, t)
            for n in range(len(owns)):
                g = low + n
                dx, dy, dz = [pos[n][a] - far_pos[a] for a in range(3)]
                inv = 1.0 / (smooth[n] + far_smooth)
                inv2 = inv * inv
                part = jnp.maximum(inv - dist[at, g, t] * inv2, 0.0)
                weight = part * part * part * inv2 * mass
                ex, ey, ez = weight * dx, weight * dy, weight * dz
                slopes[0, d, g, t], slopes[1, d, g, t], slopes[2, d, g, t] = ex, ey, ez
                for m, term in enumerate((ex * dx, ey * dy, ez * dz, ex * dy, ex * dz, ey * dz)):
                    products[m, d, g, t] = term
        return [[] for _ in owns]

    each_slot(first, count, blocks, width, cols, None, group, 2, 8)


def tensor_body(spans, groups, blocks, width, tiles, *refs):
    cols, own_rows, hot, rho = refs[:4]
    products, refs = refs[4 : 4 + len(spans)], refs[4 + len(spans) :]
    vols = refs[: 2 + groups]
    coef_out, corr_out = refs[2 + groups : 4 + groups]
    region, far_vol, result = refs[4 + groups :]

    def store(at, ref, start):
        region[pl.ds(at, SUB), :] = ref[start : start + SUB, :]

    place_region(groups, blocks, vols, SUB, region, store)
    result[...] = jnp.zeros_like(result)
    values = parts_of(region[...])
    half = tiles * SUB
    both = select(hot[...].astype(jnp.bfloat16), values)
    left, right = both[0:half], both[half:]
    far_vol[...] = jnp.where(lane_iota(half) < HALF, left, right)

    def group(product, d, at, g, own):
        total = [jnp.zeros((SUB, LANES), jnp.float32) for _ in range(6)]
        for t in range(tiles):
            weight = far_row(far_vol, 0, tiles, at, t)
            for n in range(6):
                total[n] += product[n, d, g, t] * weight
        return total

    for (first, count), product in zip(spans, products):
        each_slot(first, count, blocks, width, cols, result, functools.partial(group, product))
    sums = jnp.transpose(result[...])
    press = GAMMA_LESS * own_rows[8, :, 0:width] / rho[...]
    coefs = []
    for n in range(6):
        tensor = SLOPE * sums[n * blocks : (n + 1) * blocks, 0:width]
        corr = (2.0 + tensor) if n < 3 else tensor
        corr_out[n] = corr
        coefs.append(press * corr)
    corr_out[6] = press
    for n in range(3):
        coef_out[n * SUB : (n + 1) * SUB, :] = jnp.concatenate(coefs[2 * n : 2 * n + 2], axis=1)


def moment_body(blocks, width, tiles, spans, far, cols, *refs):
    slopes, out, result = refs[: len(spans)], refs[-2], refs[-1]
    result[...] = jnp.zeros_like(result)

    def group(slope, start, d, at, low, owns):
        vel = [[column(own, VEL + a) for a in range(3)] for own in owns]
        total = [[jnp.zeros((SUB, LANES), jnp.float32) for _ in range(9)] for _ in owns]
        for t in range(tiles):
            far_vel = [far_row(far, VEL + a, tiles, at, t) for a in range(3)]
            for k in range(len(owns)):
                px, py, pz = [slope[a, at - start, low + k, t] for a in range(3)]
                vx, vy, vz = [vel[k][a] - far_vel[a] for a in range(3)]
                terms = (
                    px,
                    py,
                    pz,
                    vx * px,
                    vy * py,
                    vz * pz,
                    vx * py + vy * px,
                    vx * pz + vz * px,
                    vy * pz + vz * py,
                )
                for n, term in enumerate(terms):
                    total[k][n] += term
        return total

    for (low, count, start), slope in zip(spans, slopes):
        each_slot(low, count, blocks, width, cols, result, functools.partial(group, slope, start), 1, 4)
    sums = jnp.transpose(result[...])
    for n in range(9):
        out[n] = sums[n * blocks : (n + 1) * blocks, 0:width]


def update_body(spans, moment_count, groups, blocks, width, tiles, *refs):
    cols, own_rows, hot, corr = refs[:4]
    slopes, refs = refs[4 : 4 + len(spans)], refs[4 + len(spans) :]
    pieces, refs = refs[:moment_count], refs[moment_count:]
    coefs = refs[: 2 + groups]
    state_out = refs[2 + groups]
    region, far_coef, result = refs[3 + groups :]

    def store(at, ref, start):
        for n in range(3):
            tile = ref[start + n * SUB : start + (n + 1) * SUB, :]
            region[pl.ds(at, SUB), n * LANES : (n + 1) * LANES] = tile

    place_region(groups, blocks, coefs, 3 * SUB, region, store)
    result[...] = jnp.zeros_like(result)
    values = parts_of(region[...])
    half = tiles * SUB
    both = select(hot[...].astype(jnp.bfloat16), values)
    left, right = both[0:half], both[half:]

    def keep(n, value):
        far_coef[n * half : (n + 1) * half, :] = value

    far_fields(left, right, keep)

    def group(slope, d, at, g, own):
        total = [jnp.zeros((SUB, LANES), jnp.float32) for _ in range(3)]
        for t in range(tiles):
            ex, ey, ez = [slope[a, d, g, t] for a in range(3)]
            xx, yy, zz, xy, xz, yz = [far_row(far_coef, n, tiles, at, t) for n in range(6)]
            total[0] += xx * ex + xy * ey + xz * ez
            total[1] += xy * ex + yy * ey + yz * ez
            total[2] += xz * ex + yz * ey + zz * ez
        return total

    for (first, count), slope in zip(spans, slopes):
        each_slot(first, count, blocks, width, cols, result, functools.partial(group, slope))
    moments = [sum(piece[m] for piece in pieces) for m in range(9)]
    sums = jnp.transpose(result[...])
    field = lambda n: own_rows[n, :, 0:width]
    live = jnp.where(lane_iota()[:, 0:width].astype(jnp.float32) < field(10), 1.0, 0.0)
    press = corr[6]
    xx, yy, zz, xy, xz, yz = [corr[n] for n in range(6)]
    sx, sy, sz = [moments[n] for n in range(3)]
    near = (xx * sx + xy * sy + xz * sz, xy * sx + yy * sy + yz * sz, xz * sx + yz * sy + zz * sz)
    for a in range(3):
        far_sum = sums[a * blocks : (a + 1) * blocks, 0:width]
        accel = -SLOPE * live * (press * near[a] + far_sum)
        velocity = field(VEL + a) + STEP_DT * accel
        state_out[3 + a] = velocity
        state_out[a] = field(X + a) + STEP_DT * velocity
    heat = moments[3] * xx + moments[4] * yy + moments[5] * zz
    heat += moments[6] * xy + moments[7] * xz + moments[8] * yz
    state_out[6] = field(9)
    state_out[7] = field(SMOOTH)
    state_out[8] = field(8) + STEP_DT * (SLOPE * live * press * heat)


def exchange(own, send_rows):
    groups = lax.axis_size("seg")
    ranges = lax.axis_size("dom")
    seg = [own]
    for k in range(1, groups):
        seg.append(lax.ppermute(own, "seg", [(i, i ^ k) for i in range(groups)]))
    whole = jnp.concatenate([part[:send_rows] for part in seg], axis=0)
    first = [(i, i ^ 1) for i in range(ranges)]
    second = []
    for r in range(ranges):
        for s in range(groups):
            inside = 0 < r < ranges - 1
            other = (((r + 1) ^ 1) - 1) * groups + s if inside else r * groups + (s ^ 1)
            second.append((r * groups + s, other))
    near = lax.ppermute(whole, "dom", first)
    beside = lax.ppermute(whole, ("dom", "seg"), second)
    return seg + [near, beside]


def spans_of(blocks, split):
    ends = [blocks * n // SUB for n in (0,) + split]
    return [(low, high - low) for low, high in zip(ends, ends[1:])]


def step(state, counts, neighbours, new_place):
    blocks, fields, width = state.shape
    nbr = neighbours.shape[1]
    groups = lax.axis_size("seg")
    slab = blocks * groups
    tiles = (nbr + 2) // 2
    size = -(-3 * slab // LANES) * LANES
    many = (blocks, width // SUB, tiles, SUB, LANES)
    f32, i32 = jnp.float32, jnp.int32
    vm = pl.BlockSpec(memory_space=VMEM)
    any_space = pl.BlockSpec(memory_space=pltpu.HBM)
    columns = VMEM((width, LANES), f32)
    packed = call(
        functools.partial(pack_body, blocks, width, nbr, tiles),
        shape(6 * SUB, LANES),
        in_specs=[any_space] * 4,
        out_specs=vm,
        scratch=(
            VMEM((fields, blocks, width), f32),
            VMEM((blocks, nbr), i32),
            SMEM((blocks,), i32),
            SMEM((blocks,), i32),
            pltpu.SemaphoreType.DMA((4,)),
        ),
    )(*[
        pltpu.with_memory_space_constraint(value, pltpu.HBM)
        for value in (counts, new_place, jnp.swapaxes(state, 0, 1), neighbours)
    ])
    parts = exchange(packed, 5 * SUB)
    cols, own_rows, hot = call(
        functools.partial(lists_body, groups, blocks, width, tiles),
        (
            shape(width, LANES),
            shape(11, SUB, LANES),
            shape(2 * tiles * SUB, size),
        ),
        in_specs=[vm] * groups,
        out_specs=(vm,) * 3,
        scratch=(VMEM((slab, 6 * LANES), f32), VMEM((LANES, LANES), f32)),
    )(*parts[:groups])
    vol, rho, far, meta, dist = call(
        functools.partial(density_body, groups, blocks, width, tiles),
        (
            shape(SUB, LANES),
            shape(blocks, width),
            shape(8 * tiles * SUB, LANES),
            shape(size, LANES),
            shape(*many),
        ),
        in_specs=[vm] * (groups + 5),
        out_specs=(vm,) * 5,
        scratch=(VMEM((size, 4 * LANES), f32), columns),
    )(cols, own_rows, hot, *parts)
    vols = exchange(vol, SUB)
    spans = spans_of(blocks, FACTOR_SPLIT)
    slopes, products = [], []
    for n, (low, count) in enumerate(spans):
        outs = (shape(3, count, *many[1:]), shape(6, count, *many[1:]))
        extra = (meta, hot) if n == 0 else ()
        if n == 0:
            outs += (shape(2 * tiles * SUB, size),)
        found = call(
            functools.partial(factor_body, low, count, blocks, slab, width, tiles),
            outs,
            in_specs=[vm] * (3 + len(extra)),
            out_specs=(vm,) * len(outs),
        )(far, cols, dist, *extra)
        slopes.append(found[0])
        products.append(found[1])
        if n == 0:
            placed = found[2]
    coef, corr = call(
        functools.partial(tensor_body, spans, groups, blocks, width, tiles),
        (shape(3 * SUB, LANES), shape(7, blocks, width)),
        in_specs=[vm] * (4 + len(spans) + groups + 2),
        out_specs=(vm, vm),
        scratch=(VMEM((size, LANES), f32), VMEM((tiles * SUB, LANES), f32), columns),
    )(cols, own_rows, placed, rho, *products, *vols)
    coefs = exchange(coef, 3 * SUB)
    moments = []
    for low, count in spans_of(blocks, MOMENT_SPLIT):
        parts, used = [], []
        for (start, length), slope in zip(spans, slopes):
            begin, end = max(low, start), min(low + count, start + length)
            if begin < end:
                parts.append((begin, end - begin, start))
                used.append(slope)
        moments.append(
            call(
                functools.partial(moment_body, blocks, width, tiles, parts),
                shape(9, blocks, width),
                in_specs=[vm] * (2 + len(used)),
                out_specs=vm,
                scratch=(columns,),
            )(far, cols, *used)
        )
    moved = call(
        functools.partial(update_body, spans, len(moments), groups, blocks, width, tiles),
        shape(fields, blocks, width),
        in_specs=[vm] * (4 + len(spans) + len(moments) + groups + 2),
        out_specs=vm,
        scratch=(
            VMEM((size, 3 * LANES), f32),
            VMEM((6 * tiles * SUB, LANES), f32),
            columns,
        ),
    )(cols, own_rows, placed, corr, *slopes, *moments, *coefs)
    return (jnp.swapaxes(moved, 0, 1), rho)


def solution(mesh):
    return jax.shard_map(
        step,
        mesh=mesh,
        in_specs=(
            P(("dom", "seg"), None, None),
            P(("dom", "seg")),
            P(("dom", "seg"), None),
            P(("dom", "seg")),
        ),
        out_specs=(P(("dom", "seg"), None, None), P(("dom", "seg"), None)),
        check_vma=False,
    )
```

```python
import functools
import math

import jax
import jax.numpy as jnp
from jax import lax
from jax.experimental import pallas as pl
from jax.experimental.pallas import tpu as pltpu
from jax.sharding import PartitionSpec as P


SIGMA = 21.0 / (16.0 * math.pi)
GAMMA_LESS = 2.0 / 3.0
STEP_DT = 0.1
SLOPE = -5.0 * SIGMA * 32.0
TINY = 1e-37
FACTOR_SPLIT = (5, 8)
MOMENT_SPLIT = (4, 8)
SUB = 8
LANES = 128
X, SMOOTH, MASS, VEL = 0, 3, 4, 5
HALF = LANES // 2
VMEM = pltpu.VMEM
SMEM = pltpu.SMEM


def lane_iota(rows=SUB):
    return lax.broadcasted_iota(jnp.int32, (rows, LANES), 1)


def row_iota(rows=SUB):
    return lax.broadcasted_iota(jnp.int32, (rows, LANES), 0)


def call(body, outs, scratch=(), in_specs=None, out_specs=None, grant=8):
    return pl.pallas_call(
        body,
        out_shape=outs,
        in_specs=in_specs,
        out_specs=out_specs,
        scratch_shapes=list(scratch),
        compiler_params=pltpu.CompilerParams(vmem_limit_bytes=grant << 20),
    )


def shape(*dims, dtype=jnp.float32):
    return jax.ShapeDtypeStruct(dims, dtype)


def pack_body(blocks, width, nbr, tiles, *refs):
    counts, place, state, lists, out, held, entries, few, ids, sem = refs
    copies = [
        pltpu.make_async_copy(source, target, sem.at[n])
        for n, (source, target) in enumerate(
            ((state, held), (lists, entries), (counts, few), (place, ids))
        )
    ]
    for copy in copies:
        copy.start()
    for copy in copies:
        copy.wait()
    groups = lax.axis_size("seg")
    me = lax.axis_index("seg")
    lane, row = lane_iota(), row_iota()
    count = jnp.zeros((SUB, LANES), jnp.int32)
    spot = jnp.zeros((SUB, LANES), jnp.int32)
    for b in range(blocks):
        count = jnp.where(row == b, few[b], count)
        spot = jnp.where(row == b, ids[b], spot)
    listed = jnp.concatenate(
        [entries[...], jnp.zeros((blocks, LANES - nbr), jnp.int32)], axis=1
    ).astype(jnp.float32)
    listed = pltpu.roll(listed, 1, axis=1)
    own = (groups * blocks + me * blocks + row).astype(jnp.float32)
    meta = jnp.where(lane == 0, own, jnp.where(lane <= nbr, listed, -1.0))
    meta = jnp.where(lane == 2 * tiles, spot.astype(jnp.float32), meta)
    meta = jnp.where(lane == 2 * tiles + 1, count.astype(jnp.float32), meta)
    rows = [held[n] for n in range(9)]
    mass = jnp.where(lane[:, 0:width] < count[:, 0:width], rows[6], 0.0)
    order = (rows[0], rows[1], rows[2], rows[7], mass, rows[3], rows[4], rows[5])
    for n in range(4):
        out[n * SUB : (n + 1) * SUB, :] = jnp.concatenate(order[2 * n : 2 * n + 2], axis=1)
    out[4 * SUB : 5 * SUB, :] = meta
    out[5 * SUB : 6 * SUB, :] = jnp.concatenate([rows[8], rows[6]], axis=1)


def place_region(groups, blocks, refs, rows, region, store):
    slab = groups * blocks
    me = lax.axis_index("seg")
    odd = lax.rem(lax.axis_index("dom"), 2)
    base_first = jnp.where(odd == 0, 2 * slab, 0)
    base_second = jnp.where(odd == 0, 0, 2 * slab)
    for k in range(groups):
        s = jnp.bitwise_xor(me, k)
        for base, ref, start in (
            (slab, refs[k], 0),
            (base_first, refs[groups], k * rows),
            (base_second, refs[groups + 1], k * rows),
        ):
            store(pl.multiple_of(base + s * blocks, SUB), ref, start)
    at_end = (lax.axis_index("dom") == 0) | (lax.axis_index("dom") == lax.axis_size("dom") - 1)

    @pl.when(at_end)
    def _():
        rows = pl.ds(pl.multiple_of(base_second, SUB), slab)
        region[rows, :] = jnp.zeros((slab, region.shape[1]), jnp.float32)

    clear_tail(region, 3 * slab)


def clear_tail(ref, first):
    if ref.shape[0] > first:
        ref[first:, :] = jnp.zeros((ref.shape[0] - first, ref.shape[1]), jnp.float32)


def parts_of(value):
    high = value.astype(jnp.bfloat16)
    rest = value - high.astype(jnp.float32)
    mid = rest.astype(jnp.bfloat16)
    return high, mid, (rest - mid.astype(jnp.float32)).astype(jnp.bfloat16)


def select(onehot, parts):
    total = None
    for part in reversed(parts):
        term = jnp.dot(onehot, part, preferred_element_type=jnp.float32)
        total = term if total is None else total + term
    return total


def far_fields(left, right, store):
    low = lane_iota(left.shape[0]) < HALF
    for n in range(left.shape[1] // LANES):
        one, two = left[:, n * LANES : (n + 1) * LANES], right[:, n * LANES : (n + 1) * LANES]
        store(2 * n, jnp.where(low, one, pltpu.roll(two, HALF, axis=1)))
        store(2 * n + 1, jnp.where(low, pltpu.roll(one, HALF, axis=1), two))


def column(value, index):
    at = index * SUB
    return jnp.broadcast_to(value[:, at : at + 1], (SUB, LANES))


def group_rows(g):
    return slice(g * SUB, (g + 1) * SUB)


def far_row(ref, field, tiles, d, t):
    return jnp.broadcast_to(ref[pl.ds((field * tiles + t) * SUB + d, 1), :], (SUB, LANES))


def each_slot(first, count, blocks, width, cols, result, group, together=2, batch=1):
    lane = lane_iota()

    def body(start, together):
        found = [[] for _ in range(width // SUB)]
        for n in range(together):
            d = start + n
            at = first + d
            own = pltpu.roll(cols[...], lax.rem(LANES - at, LANES), axis=1)
            for low in range(0, width // SUB, batch):
                rows = [own[group_rows(low + n), :] for n in range(batch)]
                if batch == 1:
                    values = [group(d, at, low, rows[0])]
                else:
                    values = group(d, at, low, rows)
                for n, totals in enumerate(values):
                    for m, value in enumerate(totals):
                        total = jnp.sum(value, axis=1, keepdims=True)
                        found[low + n].append((m * blocks + at, total))
        for g in range(width // SUB):
            if found[g]:
                rows = result[group_rows(g), :]
                for at, total in found[g]:
                    rows = jnp.where(lane == at, total, rows)
                result[group_rows(g), :] = rows

    def step(i, carry):
        body(i * together, together)
        return carry

    lax.fori_loop(0, count // together, step, 0)
    if count % together:
        body(count - count % together, count % together)


def sums_of(result, n, blocks, width):
    return jnp.transpose(result[...])[n * blocks : (n + 1) * blocks, 0:width]


def lists_body(groups, blocks, width, tiles, *refs):
    parts = refs[:groups]
    cols, own_rows, hot, own_range, own_tiles = refs[groups:]
    slab = groups * blocks
    me = lax.axis_index("seg")
    for k in range(groups):
        rows = pl.ds(pl.multiple_of(jnp.bitwise_xor(me, k) * blocks, SUB), SUB)
        for n in range(6):
            own_range[rows, n * LANES : (n + 1) * LANES] = parts[k][n * SUB : (n + 1) * SUB, :]
    own_tiles[...] = jnp.zeros_like(own_tiles)
    places = own_range[:, 4 * LANES + 2 * tiles : 4 * LANES + 2 * tiles + 1].astype(jnp.int32)
    wanted = me * blocks + lane_iota(slab)
    picks = jnp.where(jnp.broadcast_to(places, (slab, LANES)) == wanted, 1.0, 0.0)
    if slab < LANES:
        picks = jnp.concatenate([picks, jnp.zeros((LANES - slab, LANES), jnp.float32)], axis=0)
    picks = jnp.transpose(picks)[0:blocks, 0:slab].astype(jnp.bfloat16)
    mine = select(picks, parts_of(own_range[...]))
    entries = mine[:, 4 * LANES : 5 * LANES]
    for n in range(6):
        tile = mine[:, n * LANES : (n + 1) * LANES]
        if n == 4:
            continue
        at = 2 * n if n < 4 else 8
        own_rows[at] = tile
        own_rows[at + 1] = pltpu.roll(tile, HALF, axis=1)
    own_rows[10] = jnp.broadcast_to(entries[:, 2 * tiles + 1 : 2 * tiles + 2], (SUB, LANES))
    for n in range(8):
        own_tiles[n * SUB : (n + 1) * SUB, :] = own_rows[n]
    cols[...] = jnp.transpose(own_tiles[...])[0:width, :]
    size = hot.shape[1]
    column_ids = lax.broadcasted_iota(jnp.int32, (SUB, size), 1)
    index = entries.astype(jnp.int32)
    for n in range(2 * tiles):
        chosen = jnp.broadcast_to(index[:, n : n + 1], (SUB, size)) == column_ids
        hot[n * SUB : (n + 1) * SUB, :] = jnp.where(chosen, 1.0, 0.0)


def density_body(groups, blocks, width, tiles, *refs):
    cols, own_rows, hot = refs[:3]
    parts = refs[3 : groups + 5]
    vol_out, rho_out, far, meta, dist_out, region, result = refs[groups + 5 :]
    slab = groups * blocks
    kept = parts[groups].shape[0] // groups

    def store(at, ref, start):
        rows = pl.ds(at, SUB)
        for n in range(4):
            region[rows, n * LANES : (n + 1) * LANES] = ref[start + n * SUB : start + (n + 1) * SUB, :]
        meta[rows, :] = ref[start + 4 * SUB : start + 5 * SUB, :]

    place_region(groups, blocks, parts, kept, region, store)
    clear_tail(meta, 3 * slab)
    result[...] = jnp.zeros_like(result)
    values = parts_of(region[...])
    half = tiles * SUB
    both = select(hot[...].astype(jnp.bfloat16), values)
    left, right = both[0:half], both[half:]

    def keep(n, value):
        far[n * half : (n + 1) * half, :] = value

    far_fields(left, right, keep)

    def group(d, at, low, owns):
        pos = [[column(own, X + a) for a in range(3)] for own in owns]
        scale = [0.5 / column(own, SMOOTH) for own in owns]
        total = [jnp.zeros((SUB, LANES), jnp.float32) for _ in owns]
        for t in range(tiles):
            far_pos = [far_row(far, X + a, tiles, at, t) for a in range(3)]
            mass = far_row(far, MASS, tiles, at, t)
            for n in range(len(owns)):
                dx, dy, dz = [pos[n][a] - far_pos[a] for a in range(3)]
                square = dx * dx + dy * dy + dz * dz
                dist = square * lax.rsqrt(jnp.maximum(square, TINY))
                dist_out[at, low + n, t] = dist
                ratio = dist * scale[n]
                shell = jnp.maximum(1.0 - ratio, 0.0)
                shell = shell * shell
                shell = shell * shell
                total[n] += shell * (mass * (0.25 + ratio))
        return [[value] for value in total]

    each_slot(0, blocks, blocks, width, cols, result, group, 2, 4)
    sums = sums_of(result, 0, blocks, width)
    smooth, count = [own_rows[n, :, 0:width] for n in (SMOOTH, 10)]
    live = jnp.where(lane_iota()[:, 0:width].astype(jnp.float32) < count, 1.0, 0.0)
    rho = 4.0 * SIGMA / (smooth * smooth * smooth) * sums + (1.0 - live)
    rho_out[...] = rho
    share = 1.0 / rho
    vol_out[...] = jnp.concatenate([share, share], axis=1)


def placed_lists(slab, tiles, meta, hot):
    size = hot.shape[1]
    spot = meta[:, 2 * tiles : 2 * tiles + 1].astype(jnp.int32)
    rows = lax.broadcasted_iota(jnp.int32, (size, size), 0)
    start = jnp.where(rows < slab, 0, jnp.where(rows < 2 * slab, slab, 2 * slab))
    chosen = start + spot == lax.broadcasted_iota(jnp.int32, (size, size), 1)
    moves = jnp.where(chosen, 1.0, 0.0).astype(jnp.bfloat16)
    return jnp.dot(hot[...].astype(jnp.bfloat16), moves, preferred_element_type=jnp.float32)


def factor_body(first, count, blocks, slab, width, tiles, *refs):
    far, cols, dist = refs[:3]
    if first == 0:
        meta, hot = refs[3:5]
        refs[-1][...] = placed_lists(slab, tiles, meta, hot)
        slopes, products = refs[5:7]
    else:
        slopes, products = refs[3:5]

    def group(d, at, low, owns):
        pos = [[column(own, X + a) for a in range(3)] for own in owns]
        smooth = [column(own, SMOOTH) for own in owns]
        for t in range(tiles):
            far_pos = [far_row(far, X + a, tiles, at, t) for a in range(3)]
            far_smooth = far_row(far, SMOOTH, tiles, at, t)
            mass = far_row(far, MASS, tiles, at, t)
            for n in range(len(owns)):
                g = low + n
                dx, dy, dz = [pos[n][a] - far_pos[a] for a in range(3)]
                inv = 1.0 / (smooth[n] + far_smooth)
                inv2 = inv * inv
                part = jnp.maximum(inv - dist[at, g, t] * inv2, 0.0)
                weight = part * part * part * inv2 * mass
                ex, ey, ez = weight * dx, weight * dy, weight * dz
                slopes[0, d, g, t], slopes[1, d, g, t], slopes[2, d, g, t] = ex, ey, ez
                for m, term in enumerate((ex * dx, ey * dy, ez * dz, ex * dy, ex * dz, ey * dz)):
                    products[m, d, g, t] = term
        return [[] for _ in owns]

    each_slot(first, count, blocks, width, cols, None, group, 2, 8)


def tensor_body(spans, groups, blocks, width, tiles, *refs):
    cols, own_rows, hot, rho = refs[:4]
    products, refs = refs[4 : 4 + len(spans)], refs[4 + len(spans) :]
    vols = refs[: 2 + groups]
    coef_out, corr_out = refs[2 + groups : 4 + groups]
    region, far_vol, result = refs[4 + groups :]

    def store(at, ref, start):
        region[pl.ds(at, SUB), :] = ref[start : start + SUB, :]

    place_region(groups, blocks, vols, SUB, region, store)
    result[...] = jnp.zeros_like(result)
    values = parts_of(region[...])
    half = tiles * SUB
    both = select(hot[...].astype(jnp.bfloat16), values)
    left, right = both[0:half], both[half:]
    far_vol[...] = jnp.where(lane_iota(half) < HALF, left, right)

    def group(product, d, at, g, own):
        total = [jnp.zeros((SUB, LANES), jnp.float32) for _ in range(6)]
        for t in range(tiles):
            weight = far_row(far_vol, 0, tiles, at, t)
            for n in range(6):
                total[n] += product[n, d, g, t] * weight
        return total

    for (first, count), product in zip(spans, products):
        each_slot(first, count, blocks, width, cols, result, functools.partial(group, product))
    sums = jnp.transpose(result[...])
    press = GAMMA_LESS * own_rows[8, :, 0:width] / rho[...]
    coefs = []
    for n in range(6):
        tensor = SLOPE * sums[n * blocks : (n + 1) * blocks, 0:width]
        corr = (2.0 + tensor) if n < 3 else tensor
        corr_out[n] = corr
        coefs.append(press * corr)
    corr_out[6] = press
    for n in range(3):
        coef_out[n * SUB : (n + 1) * SUB, :] = jnp.concatenate(coefs[2 * n : 2 * n + 2], axis=1)


def moment_body(blocks, width, tiles, spans, far, cols, *refs):
    slopes, out, result = refs[: len(spans)], refs[-2], refs[-1]
    result[...] = jnp.zeros_like(result)

    def group(slope, start, d, at, low, owns):
        vel = [[column(own, VEL + a) for a in range(3)] for own in owns]
        total = [[jnp.zeros((SUB, LANES), jnp.float32) for _ in range(9)] for _ in owns]
        for t in range(tiles):
            far_vel = [far_row(far, VEL + a, tiles, at, t) for a in range(3)]
            for k in range(len(owns)):
                px, py, pz = [slope[a, at - start, low + k, t] for a in range(3)]
                vx, vy, vz = [vel[k][a] - far_vel[a] for a in range(3)]
                terms = (
                    px,
                    py,
                    pz,
                    vx * px,
                    vy * py,
                    vz * pz,
                    vx * py + vy * px,
                    vx * pz + vz * px,
                    vy * pz + vz * py,
                )
                for n, term in enumerate(terms):
                    total[k][n] += term
        return total

    for (low, count, start), slope in zip(spans, slopes):
        each_slot(low, count, blocks, width, cols, result, functools.partial(group, slope, start), 1, 4)
    sums = jnp.transpose(result[...])
    for n in range(9):
        out[n] = sums[n * blocks : (n + 1) * blocks, 0:width]


def update_body(spans, moment_count, groups, blocks, width, tiles, *refs):
    cols, own_rows, hot, corr = refs[:4]
    slopes, refs = refs[4 : 4 + len(spans)], refs[4 + len(spans) :]
    pieces, refs = refs[:moment_count], refs[moment_count:]
    coefs = refs[: 2 + groups]
    state_out = refs[2 + groups]
    region, far_coef, result = refs[3 + groups :]

    def store(at, ref, start):
        for n in range(3):
            tile = ref[start + n * SUB : start + (n + 1) * SUB, :]
            region[pl.ds(at, SUB), n * LANES : (n + 1) * LANES] = tile

    place_region(groups, blocks, coefs, 3 * SUB, region, store)
    result[...] = jnp.zeros_like(result)
    values = parts_of(region[...])
    half = tiles * SUB
    both = select(hot[...].astype(jnp.bfloat16), values)
    left, right = both[0:half], both[half:]

    def keep(n, value):
        far_coef[n * half : (n + 1) * half, :] = value

    far_fields(left, right, keep)

    def group(slope, d, at, low, owns):
        total = [[jnp.zeros((SUB, LANES), jnp.float32) for _ in range(3)] for _ in owns]
        for t in range(tiles):
            xx, yy, zz, xy, xz, yz = [far_row(far_coef, n, tiles, at, t) for n in range(6)]
            for k in range(len(owns)):
                ex, ey, ez = [slope[a, d, low + k, t] for a in range(3)]
                total[k][0] += xx * ex + xy * ey + xz * ez
                total[k][1] += xy * ex + yy * ey + yz * ez
                total[k][2] += xz * ex + yz * ey + zz * ez
        return total

    for (first, count), slope in zip(spans, slopes):
        each_slot(first, count, blocks, width, cols, result, functools.partial(group, slope), 2, 8)
    moments = [sum(piece[m] for piece in pieces) for m in range(9)]
    sums = jnp.transpose(result[...])
    field = lambda n: own_rows[n, :, 0:width]
    live = jnp.where(lane_iota()[:, 0:width].astype(jnp.float32) < field(10), 1.0, 0.0)
    press = corr[6]
    xx, yy, zz, xy, xz, yz = [corr[n] for n in range(6)]
    sx, sy, sz = [moments[n] for n in range(3)]
    near = (xx * sx + xy * sy + xz * sz, xy * sx + yy * sy + yz * sz, xz * sx + yz * sy + zz * sz)
    for a in range(3):
        far_sum = sums[a * blocks : (a + 1) * blocks, 0:width]
        accel = -SLOPE * live * (press * near[a] + far_sum)
        velocity = field(VEL + a) + STEP_DT * accel
        state_out[3 + a] = velocity
        state_out[a] = field(X + a) + STEP_DT * velocity
    heat = moments[3] * xx + moments[4] * yy + moments[5] * zz
    heat += moments[6] * xy + moments[7] * xz + moments[8] * yz
    state_out[6] = field(9)
    state_out[7] = field(SMOOTH)
    state_out[8] = field(8) + STEP_DT * (SLOPE * live * press * heat)


def exchange(own, send_rows):
    groups = lax.axis_size("seg")
    ranges = lax.axis_size("dom")
    seg = [own]
    for k in range(1, groups):
        seg.append(lax.ppermute(own, "seg", [(i, i ^ k) for i in range(groups)]))
    whole = jnp.concatenate([part[:send_rows] for part in seg], axis=0)
    first = [(i, i ^ 1) for i in range(ranges)]
    second = []
    for r in range(ranges):
        for s in range(groups):
            inside = 0 < r < ranges - 1
            other = (((r + 1) ^ 1) - 1) * groups + s if inside else r * groups + (s ^ 1)
            second.append((r * groups + s, other))
    near = lax.ppermute(whole, "dom", first)
    beside = lax.ppermute(whole, ("dom", "seg"), second)
    return seg + [near, beside]


def spans_of(blocks, split):
    ends = [blocks * n // SUB for n in (0,) + split]
    return [(low, high - low) for low, high in zip(ends, ends[1:])]


def step(state, counts, neighbours, new_place):
    blocks, fields, width = state.shape
    nbr = neighbours.shape[1]
    groups = lax.axis_size("seg")
    slab = blocks * groups
    tiles = (nbr + 2) // 2
    size = -(-3 * slab // LANES) * LANES
    many = (blocks, width // SUB, tiles, SUB, LANES)
    f32, i32 = jnp.float32, jnp.int32
    vm = pl.BlockSpec(memory_space=VMEM)
    any_space = pl.BlockSpec(memory_space=pltpu.HBM)
    columns = VMEM((width, LANES), f32)
    packed = call(
        functools.partial(pack_body, blocks, width, nbr, tiles),
        shape(6 * SUB, LANES),
        in_specs=[any_space] * 4,
        out_specs=vm,
        scratch=(
            VMEM((fields, blocks, width), f32),
            VMEM((blocks, nbr), i32),
            SMEM((blocks,), i32),
            SMEM((blocks,), i32),
            pltpu.SemaphoreType.DMA((4,)),
        ),
    )(*[
        pltpu.with_memory_space_constraint(value, pltpu.HBM)
        for value in (counts, new_place, jnp.swapaxes(state, 0, 1), neighbours)
    ])
    parts = exchange(packed, 5 * SUB)
    cols, own_rows, hot = call(
        functools.partial(lists_body, groups, blocks, width, tiles),
        (
            shape(width, LANES),
            shape(11, SUB, LANES),
            shape(2 * tiles * SUB, size),
        ),
        in_specs=[vm] * groups,
        out_specs=(vm,) * 3,
        scratch=(VMEM((slab, 6 * LANES), f32), VMEM((LANES, LANES), f32)),
    )(*parts[:groups])
    vol, rho, far, meta, dist = call(
        functools.partial(density_body, groups, blocks, width, tiles),
        (
            shape(SUB, LANES),
            shape(blocks, width),
            shape(8 * tiles * SUB, LANES),
            shape(size, LANES),
            shape(*many),
        ),
        in_specs=[vm] * (groups + 5),
        out_specs=(vm,) * 5,
        scratch=(VMEM((size, 4 * LANES), f32), columns),
    )(cols, own_rows, hot, *parts)
    vols = exchange(vol, SUB)
    spans = spans_of(blocks, FACTOR_SPLIT)
    slopes, products = [], []
    for n, (low, count) in enumerate(spans):
        outs = (shape(3, count, *many[1:]), shape(6, count, *many[1:]))
        extra = (meta, hot) if n == 0 else ()
        if n == 0:
            outs += (shape(2 * tiles * SUB, size),)
        found = call(
            functools.partial(factor_body, low, count, blocks, slab, width, tiles),
            outs,
            in_specs=[vm] * (3 + len(extra)),
            out_specs=(vm,) * len(outs),
        )(far, cols, dist, *extra)
        slopes.append(found[0])
        products.append(found[1])
        if n == 0:
            placed = found[2]
    coef, corr = call(
        functools.partial(tensor_body, spans, groups, blocks, width, tiles),
        (shape(3 * SUB, LANES), shape(7, blocks, width)),
        in_specs=[vm] * (4 + len(spans) + groups + 2),
        out_specs=(vm, vm),
        scratch=(VMEM((size, LANES), f32), VMEM((tiles * SUB, LANES), f32), columns),
    )(cols, own_rows, placed, rho, *products, *vols)
    coefs = exchange(coef, 3 * SUB)
    moments = []
    for low, count in spans_of(blocks, MOMENT_SPLIT):
        parts, used = [], []
        for (start, length), slope in zip(spans, slopes):
            begin, end = max(low, start), min(low + count, start + length)
            if begin < end:
                parts.append((begin, end - begin, start))
                used.append(slope)
        moments.append(
            call(
                functools.partial(moment_body, blocks, width, tiles, parts),
                shape(9, blocks, width),
                in_specs=[vm] * (2 + len(used)),
                out_specs=vm,
                scratch=(columns,),
            )(far, cols, *used)
        )
    moved = call(
        functools.partial(update_body, spans, len(moments), groups, blocks, width, tiles),
        shape(fields, blocks, width),
        in_specs=[vm] * (4 + len(spans) + len(moments) + groups + 2),
        out_specs=vm,
        scratch=(
            VMEM((size, 3 * LANES), f32),
            VMEM((6 * tiles * SUB, LANES), f32),
            columns,
        ),
    )(cols, own_rows, placed, corr, *slopes, *moments, *coefs)
    return (jnp.swapaxes(moved, 0, 1), rho)


def solution(mesh):
    return jax.shard_map(
        step,
        mesh=mesh,
        in_specs=(
            P(("dom", "seg"), None, None),
            P(("dom", "seg")),
            P(("dom", "seg"), None),
            P(("dom", "seg")),
        ),
        out_specs=(P(("dom", "seg"), None, None), P(("dom", "seg"), None)),
        check_vma=False,
    )
```
